128 devices in a mesh: rep: 16 (over z_hi, x, core), sp: 8 (over z_lo, y).
Axes of the slice: x: 4, y: 4, z: 4 (z_hi: 2, z_lo: 2; z = z_hi * 2 + z_lo), core: 2. Of those that a mesh axis runs over, the one named last changes fastest.
Arguments:
- positions: float32 [16, 3, 65536], P('rep', None, 'sp'), may hold values from -18 to 18
- velocities: float32 [16, 3, 65536], P('rep', None, 'sp'), may hold values from -6 to 6
- strength: float32 [16, 65536], P('rep', 'sp'), may hold values from 0.5 to 2
- inv_mass: float32 [16, 65536], P('rep', 'sp'), may hold values from 0.1 to 1
- tile_lists: int32 [16, 4, 512, 4], P('rep', None, 'sp'), may hold values from 0 to 127, as said below
- solute_index: int32 [16, 2048], P('rep', 'sp'), may hold values from 0 to 8191, as said below
- scatter_weight: float32 [16, 2048], P('rep', 'sp'), may hold values from 0.3 to 3
- intensity_exp: float32 [48], replicated, may hold values from 0.5 to 3
- precision: float32 [48], replicated, may hold values from 1 to 4
Outputs:
- positions_out: float32 [16, 3, 65536], P('rep', None, 'sp')
- velocities_out: float32 [16, 3, 65536], P('rep', None, 'sp')
The draws below stay inside these ranges and needn't reach their ends.
Inputs may be any that keep to these rules, and one draw needn't show every extreme that they name: `tile_lists`: for each replica, step and local block b of a domain (numbered 0 to 63), the 4 entries are distinct extended block numbers from b to b + 64, among them b, b + 32 and b + 64. `solute_index`: within each replica and domain the 256 entries are distinct local atom numbers.
All inputs are finite; a program needn't handle non-finite values.
Results may differ from the reference program's by a relative error of at most 0.0001.
Values sent between devices are 32-bit elements; how exact they have to be, the bound alone decides.
No kernel may reach another device: no remote copies, remote signals or barrier semaphores. Data moves between devices by JAX's collectives and lax.ppermute only.
A program may use at most 128 MiB of HBM per device.

```python
import math
import jax
import jax.numpy as jnp
from jax import lax

ATOM_DEV = 8192
SOL_DEV = 256
NQ = 48
M = 784
K = 4
BLOCK = 128
OUTER = 2
INNER = 2
STEPS = 4
NB = 64
HB = 32
HALO = 4096
REPLICAS = 16
ATOMS = 65536
NBLK = 512
SOL_ALL = 2048


def draw_tile_lists(key, part):
    grid_shape = (REPLICAS, STEPS, NBLK)
    local_block = jnp.arange(NBLK, dtype=jnp.int32) % NB
    inner_count = 2 * HB - 2
    steps_below = jnp.arange(1, HB, dtype=jnp.int32)
    offsets = jnp.concatenate([-steps_below[::-1], steps_below])
    scores = jax.random.randint(key, grid_shape + (inner_count,), 0, 1 << 20) * inner_count + jnp.arange(inner_count, dtype=jnp.int32)
    ranked = jnp.argsort(scores, axis=-1, stable=True)[..., :K - 3]
    chosen = offsets[ranked]
    fixed_part = jnp.broadcast_to(jnp.array([0, -HB, HB], jnp.int32), grid_shape + (3,))
    entries = jnp.concatenate([fixed_part, chosen], axis=-1)
    return (entries + HB + local_block[None, None, :, None]).astype(jnp.int32)


def draw_solute_index(key, part):
    domains = SOL_ALL // SOL_DEV
    first_key = jax.random.fold_in(key, 11)
    second_key = jax.random.fold_in(key, 23)
    atom_ids = jnp.arange(ATOM_DEV, dtype=jnp.int32)
    scores = jax.random.randint(first_key, (REPLICAS, domains, ATOM_DEV), 0, 1 << 14) * ATOM_DEV + atom_ids
    scores = jnp.where(atom_ids == 0, -2, jnp.where(atom_ids == ATOM_DEV - 1, -1, scores))
    ranked = jnp.argsort(scores, axis=-1, stable=True)[..., :SOL_DEV].astype(jnp.int32)
    shuffle_scores = jax.random.randint(second_key, (REPLICAS, domains, SOL_DEV), 0, 1 << 14) * SOL_DEV + jnp.arange(SOL_DEV, dtype=jnp.int32)
    order_index = jnp.argsort(shuffle_scores, axis=-1, stable=True)
    picked = jnp.take_along_axis(ranked, order_index, axis=-1)
    return picked.reshape(REPLICAS, domains * SOL_DEV).astype(jnp.int32)


def level_of(stream_key, shape, shards, low, top_value):
    def one(dim, shards_of):
        steps = jax.random.uniform(jax.random.fold_in(jax.random.fold_in(stream_key, 6), dim), (shards_of,), jnp.float32, low / len(shards), top_value / len(shards))
        return jnp.repeat(jnp.exp(steps), shape[dim] // shards_of).reshape((-1,) + (1,) * (len(shape) - dim - 1))

    gain = one(*shards[0])
    for cut in shards[1:]:
        gain = gain * one(*cut)
    return gain


def bell_draw(key, dims, width, reach, shards=(), held_as=jnp.bfloat16):
    drawn = jax.random.normal(key, dims, jnp.float32) * width
    if len(shards) > 0:
        drawn = level_of(key, dims, shards, -0.22, 0.18) * drawn
    return jnp.clip(drawn, min=-reach, max=reach).astype(held_as)


def setup_inputs(seed: int = 0) -> dict:
    key_of = jax.random.split(jax.random.key(seed), 10)
    return {
        "positions": bell_draw(key_of[0], (REPLICAS, 3, ATOMS), 3.0, 18.0, ((0, 16), (2, 8)), jnp.float32),
        "velocities": bell_draw(key_of[1], (REPLICAS, 3, ATOMS), 1.0, 6.0, ((0, 16), (2, 8)), jnp.float32),
        "strength": jnp.clip(jnp.exp(math.log(2.0) - 1.3862944 * jax.random.uniform(key_of[2], (REPLICAS, ATOMS), jnp.float32) ** level_of(key_of[2], (REPLICAS, ATOMS), ((0, 16), (1, 8)), -0.2, 0.2)), 0.5, 2.0),
        "inv_mass": jnp.clip(jnp.exp(math.log(1.0) - 2.3025851 * jax.random.uniform(key_of[3], (REPLICAS, ATOMS), jnp.float32) ** level_of(key_of[3], (REPLICAS, ATOMS), ((0, 16), (1, 8)), -0.2, 0.2)), 0.1, 1.0),
        "tile_lists": draw_tile_lists(jax.random.fold_in(key_of[9], 71), 0),
        "solute_index": draw_solute_index(jax.random.fold_in(key_of[9], 71), 0),
        "scatter_weight": jnp.clip(jnp.exp(math.log(3.0) - 2.3025851 * jax.random.uniform(key_of[6], (REPLICAS, SOL_ALL), jnp.float32) ** level_of(key_of[6], (REPLICAS, SOL_ALL), ((0, 16), (1, 8)), -0.2, 0.2)), 0.3, 3.0),
        "intensity_exp": jnp.clip(jax.random.uniform(key_of[7], (NQ,), jnp.float32, 0.5, 3.0), 0.5, 3.0),
        "precision": jnp.clip(jnp.exp(jax.random.uniform(key_of[8], (NQ,), jnp.float32, math.log(1.0), math.log(4.0))), 1.0, 4.0),
    }


TIME_STEP = 0.05
PAIR_STRENGTH = 0.2
HALF_INVERSE = 0.03125
shell_batch = 8
group_limit = 8

def directions(total_terms):
    order_index = jnp.arange(total_terms, dtype=jnp.int32)
    height = 1.0 - (2.0 * order_index.astype(jnp.float32) + 1.0) / total_terms
    radius = jnp.sqrt(1.0 - height * height)
    azimuth = (order_index * 610 % 987).astype(jnp.float32) * (2.0 * math.pi / 987.0)
    return (radius * jnp.cos(azimuth), radius * jnp.sin(azimuth), height)

def shell_values(total_shells):
    return 1.0 + 3.0 * jnp.arange(total_shells, dtype=jnp.int32).astype(jnp.float32) / total_shells

def projection(points, dir_x, dir_y, dir_z):
    return dir_x[:, None] * points[0][None, :] + dir_y[:, None] * points[1][None, :] + dir_z[:, None] * points[2][None, :]

def amplitude_terms(project, weights, shell_q):
    shell_blocks = shell_q.reshape(-1, shell_batch)

    def one_block(shell_block):
        phases = shell_block[:, None, None] * project[None]
        return jnp.stack([lax.optimization_barrier(jnp.sum(weights * jnp.cos(phases), axis=-1)), lax.optimization_barrier(jnp.sum(weights * jnp.sin(phases), axis=-1))])
    result = lax.map(one_block, shell_blocks)
    return jnp.transpose(result, (1, 0, 2, 3)).reshape(2, -1, project.shape[0])

def shell_intensity(amplitude):
    return lax.optimization_barrier(jnp.mean(amplitude[0] * amplitude[0] + amplitude[1] * amplitude[1], axis=-1))

def scale_grad(amplitude, intensity, precision, intensity_exp, total_terms):
    coef_shell = 2.0 * precision * (intensity - intensity_exp) / total_terms
    return coef_shell[None, :, None] * amplitude

def restraint_forces(project, weights, shell_q, weight_grad, dir_x, dir_y, dir_z):
    shell_blocks = shell_q.reshape(-1, shell_batch)
    grad_real = weight_grad[0].reshape(-1, shell_batch, project.shape[0])
    grad_imag = weight_grad[1].reshape(-1, shell_batch, project.shape[0])

    def add_block(running, pieces):
        shell_block, block_real, block_imag = pieces
        phases = shell_block[:, None, None] * project[None]
        block_term = lax.optimization_barrier(jnp.sum(shell_block[:, None, None] * (block_imag[:, :, None] * jnp.cos(phases) - block_real[:, :, None] * jnp.sin(phases)), axis=0))
        return (running + block_term, None)
    running, unused = lax.scan(add_block, jnp.zeros(project.shape, jnp.float32), (shell_blocks, grad_real, grad_imag))
    return jnp.stack([-weights * lax.optimization_barrier(jnp.sum(dir_x[:, None] * running, axis=0)), -weights * lax.optimization_barrier(jnp.sum(dir_y[:, None] * running, axis=0)), -weights * lax.optimization_barrier(jnp.sum(dir_z[:, None] * running, axis=0))])

def pair_group(own_rows, near_rows, coupling):
    delta_list = [own_rows[component][:, :, None] - near_rows[component][:, None, :] for component in range(3)]
    distance = delta_list[0] * delta_list[0] + delta_list[1] * delta_list[1] + delta_list[2] * delta_list[2]
    pair_weight = coupling * own_rows[3][:, :, None] * near_rows[3][:, None, :] * jnp.exp(-HALF_INVERSE * distance)
    return jnp.stack([lax.optimization_barrier(jnp.sum(pair_weight * delta, axis=-1)) for delta in delta_list])

def pair_forces(own_blocks, ext_blocks, tile_list):
    block_count, neighbours = tile_list.shape
    block_width = own_blocks.shape[2]
    group_size = min(group_limit, block_count)
    coupling = PAIR_STRENGTH / math.sqrt(neighbours * block_width)
    nearby = jnp.take(ext_blocks, tile_list.reshape(-1), axis=1).reshape(4, block_count // group_size, group_size, neighbours * block_width)
    grouped = own_blocks.reshape(4, block_count // group_size, group_size, block_width)

    def one_group(pieces):
        return pair_group(pieces[0], pieces[1], coupling)
    result = lax.map(one_group, (jnp.moveaxis(grouped, 1, 0), jnp.moveaxis(nearby, 1, 0)))
    return jnp.moveaxis(result, 0, 1).reshape(3, -1)

def take_columns(row_set, chosen):
    return jnp.take(row_set, chosen, axis=1)

def take_entries(row_set, chosen):
    return jnp.take(row_set, chosen)

def add_columns(row_set, chosen, extra):
    return row_set.at[:, chosen].add(extra)

def reference(positions, velocities, strength, inv_mass, tile_lists, solute_index, scatter_weight, intensity_exp, precision):
    dir_x, dir_y, dir_z = directions(M)
    shell_q = shell_values(NQ)
    first_block = jnp.arange(NBLK, dtype=jnp.int32) // NB * NB
    atom_base = jnp.arange(SOL_ALL, dtype=jnp.int32) // SOL_DEV * ATOM_DEV
    atom_index = (solute_index + atom_base[None, :]).astype(jnp.int32)
    scale_norm = 1.0 / math.sqrt(SOL_ALL)
    coords_now = positions
    speed_now = velocities
    mass_here = jax.vmap(take_entries)(inv_mass, atom_index)
    for outer_step in range(OUTER):
        points = jax.vmap(take_columns)(coords_now, atom_index)

        def replica_terms(pieces):
            project = projection(pieces[0], dir_x, dir_y, dir_z)
            return amplitude_terms(project, pieces[1], shell_q) * scale_norm
        amplitude = lax.map(replica_terms, (points, scatter_weight))
        intensity = lax.optimization_barrier(jnp.mean(jax.vmap(shell_intensity)(amplitude), axis=0))

        def replica_kick(pieces):
            project = projection(pieces[0], dir_x, dir_y, dir_z)
            weight_grad = scale_grad(pieces[2], intensity, precision, intensity_exp, M)
            return restraint_forces(project, pieces[1], shell_q, weight_grad, dir_x, dir_y, dir_z)
        saxs_kick = lax.map(replica_kick, (points, scatter_weight, amplitude))
        for inner_step in range(INNER):
            tile_step = (tile_lists[:, outer_step * INNER + inner_step] + first_block[None, :, None]).astype(jnp.int32)

            def replica_pairs(pieces):
                coords_rep, charge_rep, tile_rep = pieces
                rows_all = jnp.concatenate([coords_rep, charge_rep[None, :]], axis=0)
                padded = jnp.pad(rows_all, ((0, 0), (HALO, HALO)))
                return pair_forces(rows_all.reshape(4, NBLK, BLOCK), padded.reshape(4, NBLK + 2 * HB, BLOCK), tile_rep)
            pair_push = lax.map(replica_pairs, (coords_now, strength, tile_step))
            speed_now = speed_now + TIME_STEP * inv_mass[:, None, :] * pair_push
            coords_now = coords_now + TIME_STEP * speed_now
        impulse = INNER * TIME_STEP * mass_here[:, None, :] * saxs_kick
        speed_now = jax.vmap(add_columns)(speed_now, atom_index, impulse)
    return (coords_now, speed_now)
```

```python
import functools
import math

import jax
import jax.numpy as jnp
import numpy as np
from jax import lax
from jax.experimental import pallas as pl
from jax.experimental.pallas import tpu as pltpu
from jax.sharding import PartitionSpec as P

M = 784
NQ = 48
OUTER = 2
INNER = 2
TIME_STEP = 0.05
PAIR_STRENGTH = 0.2
HALF_INVERSE = 0.03125

BLOCK = 128
NB = 64
HB = 32
EXT = NB + 2 * HB
NEIGHBOURS = 4
ATOMS = NB * BLOCK
HALO = HB * BLOCK
SOL = 256
PARTS = 8
REPLICAS = 16
DIR_PART = M // PARTS
GROUPS = -(-DIR_PART // 8)
CENTERS = NQ // 3
LANE_GROUPS = PARTS * SOL // 128
CHUNK = 4
FILL_UNROLL = 16
BLOCK_UNROLL = 16

ALPHA = math.sqrt(HALF_INVERSE * math.log2(math.e))
COUPLING = PAIR_STRENGTH / math.sqrt(NEIGHBOURS * BLOCK)
NORM = 1.0 / math.sqrt(PARTS * SOL)
TURN = 1.0 / (32.0 * math.pi)

F32 = jnp.float32
BF16 = jnp.bfloat16


def direction_table():
    order = np.arange(M)
    height = 1.0 - (2.0 * order + 1.0) / M
    radius = np.sqrt(1.0 - height * height)
    azimuth = (order * 610 % 987) * (2.0 * math.pi / 987.0)
    rows = np.stack([radius * np.cos(azimuth), radius * np.sin(azimuth), height], axis=-1) * TURN
    table = np.zeros((PARTS, GROUPS * 8, 3), np.float32)
    table[:, :DIR_PART] = rows.reshape(PARTS, DIR_PART, 3)
    return table


def split3(value):
    high = value.astype(BF16).astype(F32)
    rest = value - high
    mid = rest.astype(BF16).astype(F32)
    return high, mid, rest - mid


def rows_of(shape):
    return lax.broadcasted_iota(jnp.int32, shape, 0)


def neighbour_features(cell):
    row = rows_of((8, BLOCK))
    both = jnp.concatenate([cell, cell], axis=0)
    charge = jnp.broadcast_to(cell[3:4], (8, BLOCK))
    moments = jnp.where((row & 3) == 3, charge, both * charge)
    th, tm, tl = split3(moments)
    weights = jnp.concatenate([jnp.where(row < 4, th, tm), jnp.where(row < 4, tl, 0.0)], axis=0)
    scaled = both * ALPHA
    space = row < 3
    norm = -jnp.sum(jnp.where(space, scaled * scaled, 0.0), axis=0, keepdims=True)
    h, m, l = split3(jnp.where(space, scaled, jnp.where(row == 4, norm, 0.0)))
    one = jnp.where(row == 3, 1.0, 0.0)
    mh = jnp.where(space, h, 0.0)
    near = jnp.concatenate([h + one, m + one, l + one, mh, jnp.where(space, m, 0.0), mh], axis=0)
    return near.astype(BF16), weights.astype(BF16)


def own_features(cell):
    row = rows_of((8, BLOCK))
    both = jnp.concatenate([cell, cell], axis=0)
    scaled = both * ALPHA
    space = row < 3
    norm = -jnp.sum(jnp.where(space, scaled * scaled, 0.0), axis=0, keepdims=True)
    h, m, l = split3(jnp.where(space, 2.0 * scaled, jnp.where(row == 3, norm, 0.0)))
    one = jnp.where(row == 4, 1.0, 0.0)
    mo = jnp.where(space, m, 0.0)
    own = jnp.concatenate(
        [h + one, jnp.where(space, h, m) + one, jnp.where(space, h, l) + one, mo, mo, jnp.where(space, l, 0.0)],
        axis=0,
    )
    return own.astype(BF16)


def selectors(index):
    block = lax.shift_right_logical(index, 7)
    lane = index & 127
    by_block = rows_of((NB, SOL)) == block
    by_lane = rows_of((BLOCK, SOL)) == lane
    return by_block, by_lane


def scatter_kicks(index_ref, weight_ref, kick_ref, push_ref):
    by_block, by_lane = selectors(index_ref[...])
    total = kick_ref[0]
    for part in range(1, PARTS):
        total = total + kick_ref[part]
    total = total * (weight_ref[...] * (-INNER * TIME_STEP))
    lanes = jnp.where(by_lane, 1.0, 0.0).astype(BF16)
    lanes = jnp.concatenate([lanes, lanes, lanes], axis=1)
    for c in range(3):
        parts = split3(total[c : c + 1])
        rows = jnp.concatenate([jnp.where(by_block, p, 0.0).astype(BF16) for p in parts], axis=1)
        push_ref[c] = lax.dot_general(rows, lanes, (((1,), (1,)), ((), ())), preferred_element_type=F32)


def gather_points(index_ref, weight_ref, place_ref, point_ref):
    by_block, by_lane = selectors(index_ref[...])
    lanes = jnp.where(by_lane, 1.0, 0.0).astype(BF16)
    found = []
    for c in range(3):
        total = None
        for p in split3(place_ref[c]):
            part = jnp.dot(p.astype(BF16), lanes, preferred_element_type=F32)
            total = part if total is None else total + part
        found.append(jnp.sum(jnp.where(by_block, total, 0.0), axis=0, keepdims=True))
    found.append(weight_ref[...])
    points = jnp.concatenate(found, axis=0)
    for part in range(PARTS):
        point_ref[part] = points


def block_at(b):
    return pl.ds(pl.multiple_of(b * BLOCK, BLOCK), BLOCK)


def pushed(push_ref, b):
    return jnp.concatenate([push_ref[c, pl.ds(b, 1), :] for c in range(3)], axis=0)


def pack_kernel(pos_ref, charge_ref, vel_ref, inverse_ref, index_ref, weight_ref, *refs):
    out_ref, head_ref, tail_ref, point_ref, place_ref = refs

    def one_block(b, carry):
        at = block_at(b)
        place = pos_ref[:, at]
        out_ref[:, at] = jnp.concatenate([place, charge_ref[:, at], vel_ref[:, at], inverse_ref[:, at]], axis=0)
        for c in range(3):
            place_ref[c, pl.ds(b, 1), :] = place[c : c + 1]
        return carry

    lax.fori_loop(0, NB, one_block, 0, unroll=FILL_UNROLL)
    head_ref[...] = out_ref[0:4, 0:HALO]
    tail_ref[...] = out_ref[0:4, HALO:ATOMS]
    gather_points(index_ref, weight_ref, place_ref, point_ref)


def finish_kernel(vel_ref, inverse_ref, index_ref, weight_ref, kick_ref, out_ref, push_ref):
    scatter_kicks(index_ref, weight_ref, kick_ref, push_ref)

    def one_block(b, carry):
        at = block_at(b)
        out_ref[:, at] = vel_ref[:, at] + inverse_ref[:, at] * pushed(push_ref, b)
        return carry

    lax.fori_loop(0, NB, one_block, 0, unroll=FILL_UNROLL)


def pair_kernel(step, kicked, gathers, last, *refs):
    refs = list(refs)
    tile_ref, position_ref, state_ref, left_ref, right_ref = refs[:5]
    refs = refs[5:]
    if kicked or gathers:
        index_ref, weight_ref = refs[:2]
        refs = refs[2:]
    if kicked:
        kick_ref = refs.pop(0)
    if last:
        pos_ref, vel_ref = refs[:2]
        refs = refs[2:]
    else:
        out_ref, head_ref, tail_ref = refs[:3]
        refs = refs[3:]
    if gathers:
        point_ref = refs.pop(0)
    near_ref, moment_ref, own_ref = refs[:3]
    refs = refs[3:]
    if gathers:
        place_ref = refs.pop(0)
    if kicked:
        push_ref = refs.pop(0)

    left_ok = jnp.where(position_ref[0] > 0, 1.0, 0.0)
    right_ok = jnp.where(position_ref[0] < PARTS - 1, 1.0, 0.0)
    row4 = rows_of((4, BLOCK))

    def fill(slot, cell):
        near, moments = neighbour_features(cell)
        near_ref[slot] = near.T
        moment_ref[slot] = moments

    def fill_halo(b, carry):
        at = block_at(b)
        fill(b, left_ref[:, at] * jnp.where(row4 == 3, left_ok, 1.0))
        fill(b + HB + NB, right_ref[:, at] * jnp.where(row4 == 3, right_ok, 1.0))
        return carry

    lax.fori_loop(0, HB, fill_halo, 0, unroll=FILL_UNROLL)

    def fill_own(b, carry):
        cell = state_ref[0:4, block_at(b)]
        fill(b + HB, cell)
        own_ref[b] = own_features(cell)
        return carry

    lax.fori_loop(0, NB, fill_own, 0, unroll=FILL_UNROLL)

    if kicked:
        scatter_kicks(index_ref, weight_ref, kick_ref, push_ref)

    def one_block(b, carry):
        entries = [tile_ref[step * NB * NEIGHBOURS + b * NEIGHBOURS + i] for i in range(NEIGHBOURS)]
        near = jnp.concatenate([near_ref[e] for e in entries], axis=0)
        moments = jnp.concatenate([moment_ref[e] for e in entries], axis=1)
        weight = jnp.exp2(jnp.dot(near, own_ref[b], preferred_element_type=F32))
        high = weight.astype(BF16)
        low = (weight - high.astype(F32)).astype(BF16)
        sums = jnp.dot(moments, high, preferred_element_type=F32)
        sums = sums + jnp.dot(moments, low, preferred_element_type=F32)
        sums = sums[0:4] + sums[4:8] + sums[8:12]
        at = block_at(b)
        cell = state_ref[:, at]
        place, charge, speed, inverse = cell[0:3], cell[3:4], cell[4:7], cell[7:8]
        force = (COUPLING * charge) * (place * sums[3:4] - sums[0:3])
        if kicked:
            speed = speed + inverse * pushed(push_ref, b)
        speed = speed + (TIME_STEP * inverse) * force
        place = place + TIME_STEP * speed
        if gathers:
            for c in range(3):
                place_ref[c, pl.ds(b, 1), :] = place[c : c + 1]
        if last:
            pos_ref[:, at] = place
            vel_ref[:, at] = speed
        else:
            out_ref[:, at] = jnp.concatenate([place, charge, speed, inverse], axis=0)
        return carry

    lax.fori_loop(0, NB, one_block, 0, unroll=BLOCK_UNROLL)

    if not last:
        head_ref[...] = out_ref[0:4, 0:HALO]
        tail_ref[...] = out_ref[0:4, HALO:ATOMS]
    if gathers:
        gather_points(index_ref, weight_ref, place_ref, point_ref)


VMEM = pl.BlockSpec(memory_space=pltpu.VMEM)
SMEM = pl.BlockSpec(memory_space=pltpu.SMEM)
PARAMS = pltpu.CompilerParams(vmem_limit_bytes=32 << 20)


def pack(positions, strength, velocities, inv_mass, index, weights):
    return pl.pallas_call(
        pack_kernel,
        out_shape=[
            jax.ShapeDtypeStruct((8, ATOMS), F32),
            jax.ShapeDtypeStruct((4, HALO), F32),
            jax.ShapeDtypeStruct((4, HALO), F32),
            jax.ShapeDtypeStruct((PARTS, 4, SOL), F32),
        ],
        in_specs=[VMEM] * 6,
        out_specs=[VMEM] * 4,
        scratch_shapes=[pltpu.VMEM((3, NB, BLOCK), F32)],
        compiler_params=PARAMS,
        cost_estimate=pl.CostEstimate(flops=100_000_000, bytes_accessed=600_000, transcendentals=0),
        name="pack",
    )(positions, strength, velocities, inv_mass, index, weights)


def finish(velocities, inv_mass, index, weights, kick):
    return pl.pallas_call(
        finish_kernel,
        out_shape=jax.ShapeDtypeStruct((3, ATOMS), F32),
        in_specs=[VMEM] * 5,
        out_specs=VMEM,
        scratch_shapes=[pltpu.VMEM((3, NB, BLOCK), F32)],
        compiler_params=PARAMS,
        cost_estimate=pl.CostEstimate(flops=100_000_000, bytes_accessed=300_000, transcendentals=0),
        name="finish",
    )(velocities, inv_mass, index, weights, kick)


def pair_step(step, tiles, position, state, halo, index=None, weights=None, kick=None, gathers=False, last=False):
    kicked = kick is not None
    operands = [tiles, position, state, halo[0], halo[1]]
    specs = [SMEM, SMEM, VMEM, VMEM, VMEM]
    if kicked or gathers:
        operands += [index, weights]
        specs += [VMEM, VMEM]
    if kicked:
        operands.append(kick)
        specs.append(VMEM)
    scratch = [
        pltpu.VMEM((EXT, BLOCK, 48), BF16),
        pltpu.VMEM((EXT, 16, BLOCK), BF16),
        pltpu.VMEM((NB, 48, BLOCK), BF16),
    ]
    if last:
        shapes = [jax.ShapeDtypeStruct((3, ATOMS), F32)] * 2
    else:
        shapes = [jax.ShapeDtypeStruct((8, ATOMS), F32)] + [jax.ShapeDtypeStruct((4, HALO), F32)] * 2
    if gathers:
        shapes.append(jax.ShapeDtypeStruct((PARTS, 4, SOL), F32))
        scratch.append(pltpu.VMEM((3, NB, BLOCK), F32))
    if kicked:
        scratch.append(pltpu.VMEM((3, NB, BLOCK), F32))
    return pl.pallas_call(
        functools.partial(pair_kernel, step, kicked, gathers, last),
        out_shape=shapes,
        in_specs=specs,
        out_specs=[VMEM] * len(shapes),
        scratch_shapes=scratch,
        compiler_params=PARAMS,
        cost_estimate=pl.CostEstimate(flops=6_000_000_000, bytes_accessed=2_000_000, transcendentals=4_000_000),
        name="pair_step",
    )(*operands)


def double(cos, sin):
    twice = sin + sin
    return 1.0 - twice * sin, twice * cos


def product(a, b):
    return a[0] * b[0] - a[1] * b[1], a[1] * b[0] + a[0] * b[1]


def product_conj(a, b):
    return a[0] * b[0] + a[1] * b[1], a[1] * b[0] - a[0] * b[1]


def unit_powers(turns):
    y = (turns - jnp.round(turns)) * (0.5 * math.pi)
    z = y * y
    sin = ((-1.9515295891e-4 * z + 8.3321608736e-3) * z - 1.6666654611e-1) * (z * y) + y
    cos = ((2.443315711809948e-5 * z - 1.388731625493765e-3) * z + 4.166664568298827e-2) * (z * z) + (1.0 - 0.5 * z)
    one = double(*double(cos, sin))
    two = double(*one)
    three = product(two, one)
    sixteen = double(*double(*double(*two)))
    return one, three, product(sixteen, one)


def group_turns(dir_ref, point_ref, part, half):
    lanes = slice(half * 128, half * 128 + 128)

    def coordinate(c):
        return jnp.broadcast_to(point_ref[part, c : c + 1, lanes], (8, 128))

    u = [jnp.broadcast_to(dir_ref[0, :, c : c + 1], (8, 128)) for c in range(3)]
    return u[0] * coordinate(0) + u[1] * coordinate(1) + u[2] * coordinate(2), coordinate(3)


def amplitude_kernel(position_ref, point_ref, dir_ref, amp_ref, inten_ref, acc_ref, square_ref):
    group = pl.program_id(0)
    zero = jnp.zeros((8, 128), F32)

    @pl.when(group == 0)
    def _():
        square_ref[...] = zero

    for i in range(6 * CENTERS):
        acc_ref[i] = zero

    def chunk(at, carry):
        state = []
        for n in range(CHUNK):
            turns, weight = group_turns(dir_ref, point_ref, at * (CHUNK // 2) + n // 2, n % 2)
            one, three, start = unit_powers(turns)
            now = (weight * start[0], weight * start[1])
            before = product_conj(now, three)
            state.append([one[0], one[1], three[0] + three[0], now[0], now[1], before[0], before[1]])
        for k in range(CENTERS):
            sums = None
            for n in range(CHUNK):
                c1, s1, step, c, s, cb, sb = state[n]
                terms = [c, s, c * c1, s * s1, s * c1, c * s1]
                sums = terms if sums is None else [p + q for p, q in zip(sums, terms)]
                if k + 1 < CENTERS:
                    state[n][3:] = [step * c - cb, step * s - sb, c, s]
            for i in range(6):
                acc_ref[6 * k + i] += sums[i]
        return carry

    lax.fori_loop(0, LANE_GROUPS // CHUNK, chunk, 0, unroll=True)

    lane = lax.broadcasted_iota(jnp.int32, (8, 128), 1)
    inside = rows_of((8, 128)) + group * 8 < DIR_PART
    real = zero
    imag = zero
    for k in range(CENTERS):
        c, s, t1, t2, t3, t4 = [acc_ref[6 * k + i] for i in range(6)]
        for i, (a, b) in enumerate([(t1 + t2, t3 - t4), (c, s), (t1 - t2, t3 + t4)]):
            here = lane == 16 * i + k
            real = jnp.where(here, jnp.sum(a, axis=1, keepdims=True), real)
            imag = jnp.where(here, jnp.sum(b, axis=1, keepdims=True), imag)
    real = real * NORM
    imag = imag * NORM
    amp_ref[0, 0] = real
    amp_ref[0, 1] = imag
    square_ref[...] += jnp.where(inside, real * real + imag * imag, 0.0)

    @pl.when(group == GROUPS - 1)
    def _():
        inten_ref[...] = jnp.broadcast_to(jnp.sum(square_ref[...], axis=0, keepdims=True), inten_ref.shape)


def point_spec():
    return pl.BlockSpec((PARTS, 4, SOL), lambda g, p: (0, 0, 0))


def direction_spec():
    return pl.BlockSpec((1, 8, 3), lambda g, p: (p[0], g, 0))


def amplitudes(position, points, directions):
    return pl.pallas_call(
        amplitude_kernel,
        grid_spec=pltpu.PrefetchScalarGridSpec(
            num_scalar_prefetch=1,
            grid=(GROUPS,),
            in_specs=[point_spec(), direction_spec()],
            out_specs=[
                pl.BlockSpec((1, 2, 8, 128), lambda g, p: (g, 0, 0, 0)),
                pl.BlockSpec((PARTS * REPLICAS, 128), lambda g, p: (0, 0)),
            ],
            scratch_shapes=[pltpu.VMEM((6 * CENTERS, 8, 128), F32), pltpu.VMEM((8, 128), F32)],
        ),
        out_shape=[
            jax.ShapeDtypeStruct((GROUPS, 2, 8, 128), F32),
            jax.ShapeDtypeStruct((PARTS * REPLICAS, 128), F32),
        ],
        compiler_params=PARAMS,
        cost_estimate=pl.CostEstimate(flops=10_000_000_000, bytes_accessed=1_000_000, transcendentals=0),
        name="amplitudes",
    )(position, points, directions)


def kick_kernel(position_ref, point_ref, dir_ref, amp_ref, inten_ref, shell_ref, out_ref, coef_ref, scale_ref, acc_ref):
    group = pl.program_id(0)

    @pl.when(group == 0)
    def _():
        intensity = jnp.sum(inten_ref[...], axis=0, keepdims=True) * (1.0 / (M * REPLICAS))
        lane = lax.broadcasted_iota(jnp.int32, (1, 128), 1)
        shell = 1.0 + (3 * (lane & 15) + lax.shift_right_logical(lane, 4)).astype(F32) * (3.0 / NQ)
        factor = shell_ref[0:1] * (intensity - shell_ref[1:2]) * (2.0 / M) * shell
        scale_ref[...] = jnp.broadcast_to(factor, (8, 128))
        for i in range(LANE_GROUPS * 3):
            acc_ref[i] = jnp.zeros((8, 128), F32)

    b = amp_ref[0, 0] * scale_ref[...]
    a = amp_ref[0, 1] * scale_ref[...]
    for k in range(CENTERS):
        ax = [jnp.broadcast_to(a[:, 16 * i + k : 16 * i + k + 1], (8, 128)) for i in range(3)]
        bx = [jnp.broadcast_to(b[:, 16 * i + k : 16 * i + k + 1], (8, 128)) for i in range(3)]
        for i, v in enumerate([ax[1], ax[0] + ax[2], bx[0] - bx[2], bx[1], bx[0] + bx[2], ax[2] - ax[0]]):
            coef_ref[6 * k + i] = v

    def chunk(at, carry):
        state = []
        for n in range(CHUNK):
            turns, _ = group_turns(dir_ref, point_ref, at * (CHUNK // 2) + n // 2, n % 2)
            one, three, start = unit_powers(turns)
            state.append([one, three, start, three[0] + three[0], None, None, None, None])
        for k in range(CENTERS - 1, -1, -1):
            a1, ap, bm, b1, bp, am = [coef_ref[6 * k + i] for i in range(6)]
            for n in range(CHUNK):
                one, three, start, step, r1, i1, r2, i2 = state[n]
                real = a1 + ap * one[0] + bm * one[1]
                imag = b1 + bp * one[0] + am * one[1]
                if r1 is not None:
                    real = real + step * r1
                    imag = imag + step * i1
                if r2 is not None:
                    real = real - r2
                    imag = imag - i2
                state[n][4:] = [real, imag, r1, i1]
        for n in range(CHUNK):
            one, three, start, step, r0, i0, r1, i1 = state[n]
            real = r0 - r1 * three[0] - i1 * three[1]
            imag = i0 - i1 * three[0] + r1 * three[1]
            slope = real * start[0] - imag * start[1]
            for c in range(3):
                u = jnp.broadcast_to(dir_ref[0, :, c : c + 1], (8, 128))
                acc_ref[(at * CHUNK + n) * 3 + c] += u * slope
        return carry

    lax.fori_loop(0, LANE_GROUPS // CHUNK, chunk, 0, unroll=True)

    @pl.when(group == GROUPS - 1)
    def _():
        for j in range(LANE_GROUPS):
            lanes = slice(j % 2 * 128, j % 2 * 128 + 128)
            for c in range(3):
                out_ref[j // 2, c : c + 1, lanes] = jnp.sum(acc_ref[j * 3 + c], axis=0, keepdims=True) * (1.0 / TURN)


def kicks(position, points, directions, amplitude, intensity, shells):
    return pl.pallas_call(
        kick_kernel,
        grid_spec=pltpu.PrefetchScalarGridSpec(
            num_scalar_prefetch=1,
            grid=(GROUPS,),
            in_specs=[
                point_spec(),
                direction_spec(),
                pl.BlockSpec((1, 2, 8, 128), lambda g, p: (g, 0, 0, 0)),
                pl.BlockSpec((PARTS * REPLICAS, 128), lambda g, p: (0, 0)),
                pl.BlockSpec((2, 128), lambda g, p: (0, 0)),
            ],
            out_specs=pl.BlockSpec((PARTS, 3, SOL), lambda g, p: (0, 0, 0)),
            scratch_shapes=[
                pltpu.VMEM((6 * CENTERS, 8, 128), F32),
                pltpu.VMEM((8, 128), F32),
                pltpu.VMEM((LANE_GROUPS * 3, 8, 128), F32),
            ],
        ),
        out_shape=jax.ShapeDtypeStruct((PARTS, 3, SOL), F32),
        compiler_params=PARAMS,
        cost_estimate=pl.CostEstimate(flops=10_000_000_000, bytes_accessed=1_000_000, transcendentals=0),
        name="kicks",
    )(position, points, directions, amplitude, intensity, shells)


def exchange(head, tail):
    right = [(i, (i + 1) % PARTS) for i in range(PARTS)]
    left = [((i + 1) % PARTS, i) for i in range(PARTS)]
    return lax.ppermute(tail, "sp", right), lax.ppermute(head, "sp", left)


def to_all(value, axes):
    return lax.all_to_all(value, axes, 0, 0, tiled=True)


def shards(
    positions,
    velocities,
    strength,
    inv_mass,
    tile_lists,
    solute_index,
    scatter_weight,
    intensity_exp,
    precision,
):
    position = lax.axis_index("sp").astype(jnp.int32).reshape(1)
    directions = jnp.asarray(direction_table())
    tiles = tile_lists.reshape(-1)
    shells = jnp.stack([precision, intensity_exp]).reshape(2, CENTERS, 3)
    shells = jnp.pad(jnp.swapaxes(shells, 1, 2).reshape(2, NQ), ((0, 0), (0, 128 - NQ)))
    state, head, tail, first = pack(
        positions[0], strength, velocities[0], inv_mass, solute_index, scatter_weight
    )
    halo = exchange(head, tail)
    first = to_all(first, "sp")
    state, head, tail = pair_step(0, tiles, position, state, halo)
    halo = exchange(head, tail)
    amp, inten = amplitudes(position, first, directions)
    inten = to_all(inten, ("rep", "sp"))
    state, head, tail, second = pair_step(
        1, tiles, position, state, halo, solute_index, scatter_weight, gathers=True
    )
    halo = exchange(head, tail)
    second = to_all(second, "sp")
    kick = to_all(kicks(position, first, directions, amp, inten, shells), "sp")
    amp, inten = amplitudes(position, second, directions)
    inten = to_all(inten, ("rep", "sp"))
    state, head, tail = pair_step(2, tiles, position, state, halo, solute_index, scatter_weight, kick)
    halo = exchange(head, tail)
    kick = to_all(kicks(position, second, directions, amp, inten, shells), "sp")
    place, speed = pair_step(3, tiles, position, state, halo, last=True)
    speed = finish(speed, inv_mass, solute_index, scatter_weight, kick)
    return (place[None], speed[None])


def solution(mesh):
    in_specs = (
        P("rep", None, "sp"),
        P("rep", None, "sp"),
        P("rep", "sp"),
        P("rep", "sp"),
        P("rep", None, "sp", None),
        P("rep", "sp"),
        P("rep", "sp"),
        P(),
        P(),
    )
    out_specs = (P("rep", None, "sp"), P("rep", None, "sp"))
    return jax.shard_map(shards, mesh=mesh, in_specs=in_specs, out_specs=out_specs, check_vma=False)
```

```python
import functools
import math

import jax
import jax.numpy as jnp
import numpy as np
from jax import lax
from jax.experimental import pallas as pl
from jax.experimental.pallas import tpu as pltpu
from jax.sharding import PartitionSpec as P

M = 784
NQ = 48
OUTER = 2
INNER = 2
TIME_STEP = 0.05
PAIR_STRENGTH = 0.2
HALF_INVERSE = 0.03125

BLOCK = 128
NB = 64
HB = 32
EXT = NB + 2 * HB
NEIGHBOURS = 4
ATOMS = NB * BLOCK
HALO = HB * BLOCK
SOL = 256
PARTS = 8
REPLICAS = 16
DIR_PART = M // PARTS
GROUPS = -(-DIR_PART // 8)
SIDE = 4
CENTERS = NQ // (2 * SIDE)
LANE_GROUPS = PARTS * SOL // 128
CHUNK = 4
FILL_UNROLL = 16
BLOCK_UNROLL = 16

ALPHA = math.sqrt(HALF_INVERSE * math.log2(math.e))
COUPLING = PAIR_STRENGTH / math.sqrt(NEIGHBOURS * BLOCK)
NORM = 1.0 / math.sqrt(PARTS * SOL)
TURN = 1.0 / (64.0 * math.pi)

F32 = jnp.float32
BF16 = jnp.bfloat16


def direction_table():
    order = np.arange(M)
    height = 1.0 - (2.0 * order + 1.0) / M
    radius = np.sqrt(1.0 - height * height)
    azimuth = (order * 610 % 987) * (2.0 * math.pi / 987.0)
    rows = np.stack([radius * np.cos(azimuth), radius * np.sin(azimuth), height], axis=-1) * TURN
    padded = np.zeros((PARTS, GROUPS * 8, 3), np.float32)
    padded[:, :DIR_PART] = rows.reshape(PARTS, DIR_PART, 3)
    table = np.zeros((PARTS, 8, 128), np.float32)
    for c in range(3):
        table[:, :, 16 * c : 16 * c + GROUPS] = np.swapaxes(padded[:, :, c].reshape(PARTS, GROUPS, 8), 1, 2)
    return table


def split3(value):
    high = value.astype(BF16).astype(F32)
    rest = value - high
    mid = rest.astype(BF16).astype(F32)
    return high, mid, rest - mid


def rows_of(shape):
    return lax.broadcasted_iota(jnp.int32, shape, 0)


def neighbour_features(cell):
    row = rows_of((8, BLOCK))
    both = jnp.concatenate([cell, cell], axis=0)
    charge = jnp.broadcast_to(cell[3:4], (8, BLOCK))
    moments = jnp.where((row & 3) == 3, charge, both * charge)
    th, tm, tl = split3(moments)
    weights = jnp.concatenate([jnp.where(row < 4, th, tm), jnp.where(row < 4, tl, 0.0)], axis=0)
    scaled = both * ALPHA
    space = row < 3
    norm = -jnp.sum(jnp.where(space, scaled * scaled, 0.0), axis=0, keepdims=True)
    h, m, l = split3(jnp.where(space, scaled, jnp.where(row == 4, norm, 0.0)))
    one = jnp.where(row == 3, 1.0, 0.0)
    mh = jnp.where(space, h, 0.0)
    near = jnp.concatenate([h + one, m + one, l + one, mh, jnp.where(space, m, 0.0), mh], axis=0)
    return near.astype(BF16), weights.astype(BF16)


def own_features(cell):
    row = rows_of((8, BLOCK))
    both = jnp.concatenate([cell, cell], axis=0)
    scaled = both * ALPHA
    space = row < 3
    norm = -jnp.sum(jnp.where(space, scaled * scaled, 0.0), axis=0, keepdims=True)
    h, m, l = split3(jnp.where(space, 2.0 * scaled, jnp.where(row == 3, norm, 0.0)))
    one = jnp.where(row == 4, 1.0, 0.0)
    mo = jnp.where(space, m, 0.0)
    own = jnp.concatenate(
        [h + one, jnp.where(space, h, m) + one, jnp.where(space, h, l) + one, mo, mo, jnp.where(space, l, 0.0)],
        axis=0,
    )
    return own.astype(BF16)


def selectors(index):
    block = lax.shift_right_logical(index, 7)
    lane = index & 127
    by_block = rows_of((NB, SOL)) == block
    by_lane = rows_of((BLOCK, SOL)) == lane
    return by_block, by_lane


def scatter_kicks(index_ref, weight_ref, kick_ref, push_ref):
    by_block, by_lane = selectors(index_ref[...])
    total = kick_ref[0]
    for part in range(1, PARTS):
        total = total + kick_ref[part]
    total = total * (weight_ref[...] * (-INNER * TIME_STEP))
    lanes = jnp.where(by_lane, 1.0, 0.0).astype(BF16)
    lanes = jnp.concatenate([lanes, lanes, lanes], axis=1)
    for c in range(3):
        parts = split3(total[c : c + 1])
        rows = jnp.concatenate([jnp.where(by_block, p, 0.0).astype(BF16) for p in parts], axis=1)
        push_ref[c] = lax.dot_general(rows, lanes, (((1,), (1,)), ((), ())), preferred_element_type=F32)


def gather_points(index_ref, weight_ref, place_ref, point_ref):
    by_block, by_lane = selectors(index_ref[...])
    lanes = jnp.where(by_lane, 1.0, 0.0).astype(BF16)
    found = []
    for c in range(3):
        total = None
        for p in split3(place_ref[c]):
            part = jnp.dot(p.astype(BF16), lanes, preferred_element_type=F32)
            total = part if total is None else total + part
        found.append(jnp.sum(jnp.where(by_block, total, 0.0), axis=0, keepdims=True))
    found.append(weight_ref[...])
    points = jnp.concatenate(found, axis=0)
    for part in range(PARTS):
        point_ref[part] = points


def block_at(b):
    return pl.ds(pl.multiple_of(b * BLOCK, BLOCK), BLOCK)


def pushed(push_ref, b):
    return jnp.concatenate([push_ref[c, pl.ds(b, 1), :] for c in range(3)], axis=0)


def pack_kernel(pos_ref, charge_ref, vel_ref, inverse_ref, index_ref, weight_ref, *refs):
    out_ref, head_ref, tail_ref, point_ref, place_ref = refs

    def one_block(b, carry):
        at = block_at(b)
        place = pos_ref[:, at]
        out_ref[:, at] = jnp.concatenate([place, charge_ref[:, at], vel_ref[:, at], inverse_ref[:, at]], axis=0)
        for c in range(3):
            place_ref[c, pl.ds(b, 1), :] = place[c : c + 1]
        return carry

    lax.fori_loop(0, NB, one_block, 0, unroll=FILL_UNROLL)
    head_ref[...] = out_ref[0:4, 0:HALO]
    tail_ref[...] = out_ref[0:4, HALO:ATOMS]
    gather_points(index_ref, weight_ref, place_ref, point_ref)


def finish_kernel(vel_ref, inverse_ref, index_ref, weight_ref, kick_ref, out_ref, push_ref):
    scatter_kicks(index_ref, weight_ref, kick_ref, push_ref)

    def one_block(b, carry):
        at = block_at(b)
        out_ref[:, at] = vel_ref[:, at] + inverse_ref[:, at] * pushed(push_ref, b)
        return carry

    lax.fori_loop(0, NB, one_block, 0, unroll=FILL_UNROLL)


def pair_kernel(step, kicked, gathers, last, *refs):
    refs = list(refs)
    tile_ref, position_ref, state_ref, left_ref, right_ref = refs[:5]
    refs = refs[5:]
    if kicked or gathers:
        index_ref, weight_ref = refs[:2]
        refs = refs[2:]
    if kicked:
        kick_ref = refs.pop(0)
    if last:
        pos_ref, vel_ref = refs[:2]
        refs = refs[2:]
    else:
        out_ref, head_ref, tail_ref = refs[:3]
        refs = refs[3:]
    if gathers:
        point_ref = refs.pop(0)
    near_ref, moment_ref, own_ref = refs[:3]
    refs = refs[3:]
    if gathers:
        place_ref = refs.pop(0)
    if kicked:
        push_ref = refs.pop(0)

    left_ok = jnp.where(position_ref[0] > 0, 1.0, 0.0)
    right_ok = jnp.where(position_ref[0] < PARTS - 1, 1.0, 0.0)
    row4 = rows_of((4, BLOCK))

    def fill(slot, cell):
        near, moments = neighbour_features(cell)
        near_ref[slot] = near.T
        moment_ref[slot] = moments

    def fill_halo(b, carry):
        at = block_at(b)
        fill(b, left_ref[:, at] * jnp.where(row4 == 3, left_ok, 1.0))
        fill(b + HB + NB, right_ref[:, at] * jnp.where(row4 == 3, right_ok, 1.0))
        return carry

    lax.fori_loop(0, HB, fill_halo, 0, unroll=FILL_UNROLL)

    def fill_own(b, carry):
        cell = state_ref[0:4, block_at(b)]
        fill(b + HB, cell)
        own_ref[b] = own_features(cell)
        return carry

    lax.fori_loop(0, NB, fill_own, 0, unroll=FILL_UNROLL)

    if kicked:
        scatter_kicks(index_ref, weight_ref, kick_ref, push_ref)

    def one_block(b, carry):
        entries = [tile_ref[step * NB * NEIGHBOURS + b * NEIGHBOURS + i] for i in range(NEIGHBOURS)]
        near = jnp.concatenate([near_ref[e] for e in entries], axis=0)
        moments = jnp.concatenate([moment_ref[e] for e in entries], axis=1)
        weight = jnp.exp2(jnp.dot(near, own_ref[b], preferred_element_type=F32))
        high = weight.astype(BF16)
        low = (weight - high.astype(F32)).astype(BF16)
        sums = jnp.dot(moments, high, preferred_element_type=F32)
        sums = sums + jnp.dot(moments, low, preferred_element_type=F32)
        sums = sums[0:4] + sums[4:8] + sums[8:12]
        at = block_at(b)
        cell = state_ref[:, at]
        place, charge, speed, inverse = cell[0:3], cell[3:4], cell[4:7], cell[7:8]
        force = (COUPLING * charge) * (place * sums[3:4] - sums[0:3])
        if kicked:
            speed = speed + inverse * pushed(push_ref, b)
        speed = speed + (TIME_STEP * inverse) * force
        place = place + TIME_STEP * speed
        if gathers:
            for c in range(3):
                place_ref[c, pl.ds(b, 1), :] = place[c : c + 1]
        if last:
            pos_ref[:, at] = place
            vel_ref[:, at] = speed
        else:
            out_ref[:, at] = jnp.concatenate([place, charge, speed, inverse], axis=0)
        return carry

    lax.fori_loop(0, NB, one_block, 0, unroll=BLOCK_UNROLL)

    if not last:
        head_ref[...] = out_ref[0:4, 0:HALO]
        tail_ref[...] = out_ref[0:4, HALO:ATOMS]
    if gathers:
        gather_points(index_ref, weight_ref, place_ref, point_ref)


VMEM = pl.BlockSpec(memory_space=pltpu.VMEM)
SMEM = pl.BlockSpec(memory_space=pltpu.SMEM)
PARAMS = pltpu.CompilerParams(vmem_limit_bytes=32 << 20)


def pack(positions, strength, velocities, inv_mass, index, weights):
    return pl.pallas_call(
        pack_kernel,
        out_shape=[
            jax.ShapeDtypeStruct((8, ATOMS), F32),
            jax.ShapeDtypeStruct((4, HALO), F32),
            jax.ShapeDtypeStruct((4, HALO), F32),
            jax.ShapeDtypeStruct((PARTS, 4, SOL), F32),
        ],
        in_specs=[VMEM] * 6,
        out_specs=[VMEM] * 4,
        scratch_shapes=[pltpu.VMEM((3, NB, BLOCK), F32)],
        compiler_params=PARAMS,
        cost_estimate=pl.CostEstimate(flops=100_000_000, bytes_accessed=600_000, transcendentals=0),
        name="pack",
    )(positions, strength, velocities, inv_mass, index, weights)


def finish(velocities, inv_mass, index, weights, kick):
    return pl.pallas_call(
        finish_kernel,
        out_shape=jax.ShapeDtypeStruct((3, ATOMS), F32),
        in_specs=[VMEM] * 5,
        out_specs=VMEM,
        scratch_shapes=[pltpu.VMEM((3, NB, BLOCK), F32)],
        compiler_params=PARAMS,
        cost_estimate=pl.CostEstimate(flops=100_000_000, bytes_accessed=300_000, transcendentals=0),
        name="finish",
    )(velocities, inv_mass, index, weights, kick)


def pair_step(step, tiles, position, state, halo, index=None, weights=None, kick=None, gathers=False, last=False):
    kicked = kick is not None
    operands = [tiles, position, state, halo[0], halo[1]]
    specs = [SMEM, SMEM, VMEM, VMEM, VMEM]
    if kicked or gathers:
        operands += [index, weights]
        specs += [VMEM, VMEM]
    if kicked:
        operands.append(kick)
        specs.append(VMEM)
    scratch = [
        pltpu.VMEM((EXT, BLOCK, 48), BF16),
        pltpu.VMEM((EXT, 16, BLOCK), BF16),
        pltpu.VMEM((NB, 48, BLOCK), BF16),
    ]
    if last:
        shapes = [jax.ShapeDtypeStruct((3, ATOMS), F32)] * 2
    else:
        shapes = [jax.ShapeDtypeStruct((8, ATOMS), F32)] + [jax.ShapeDtypeStruct((4, HALO), F32)] * 2
    if gathers:
        shapes.append(jax.ShapeDtypeStruct((PARTS, 4, SOL), F32))
        scratch.append(pltpu.VMEM((3, NB, BLOCK), F32))
    if kicked:
        scratch.append(pltpu.VMEM((3, NB, BLOCK), F32))
    return pl.pallas_call(
        functools.partial(pair_kernel, step, kicked, gathers, last),
        out_shape=shapes,
        in_specs=specs,
        out_specs=[VMEM] * len(shapes),
        scratch_shapes=scratch,
        compiler_params=PARAMS,
        cost_estimate=pl.CostEstimate(flops=6_000_000_000, bytes_accessed=2_000_000, transcendentals=4_000_000),
        name="pair_step",
    )(*operands)


def double(cos, sin):
    twice = sin + sin
    return 1.0 - twice * sin, twice * cos


def product(a, b):
    return a[0] * b[0] - a[1] * b[1], a[1] * b[0] + a[0] * b[1]


def product_conj(a, b):
    return a[0] * b[0] + a[1] * b[1], a[1] * b[0] - a[0] * b[1]


def unit_powers(turns):
    y = (turns - jnp.round(turns)) * (0.5 * math.pi)
    z = y * y
    sin = ((-1.9515295891e-4 * z + 8.3321608736e-3) * z - 1.6666654611e-1) * (z * y) + y
    cos = ((2.443315711809948e-5 * z - 1.388731625493765e-3) * z + 4.166664568298827e-2) * (z * z) + (1.0 - 0.5 * z)
    one = double(*double(cos, sin))
    two = double(*one)
    three = product(two, one)
    five = product(three, two)
    seven = product(five, two)
    sixteen = double(*double(*double(*two)))
    return [one, three, five, seven], sixteen, product(double(*sixteen), seven)


def halves(value):
    high = value.astype(BF16)
    return high, (value - high.astype(F32)).astype(BF16)


def term_rows(powers):
    values = [p[0] for p in powers] + [p[1] for p in powers]
    parts = [halves(jnp.concatenate(values[i : i + 2], axis=0)) for i in range(0, 8, 2)]
    return [p[0] for p in parts], [p[1] for p in parts]


def group_directions(dir_ref, group):
    lane = lax.broadcasted_iota(jnp.int32, (8, 128), 1)

    def one(c):
        column = jnp.sum(jnp.where(lane == 16 * c + group, dir_ref[0], 0.0), axis=1, keepdims=True)
        return jnp.broadcast_to(column, (8, 128))

    return [one(c) for c in range(3)]


def group_turns(u, point_ref, part, half):
    lanes = slice(half * 128, half * 128 + 128)

    def coordinate(c):
        return jnp.broadcast_to(point_ref[part, c : c + 1, lanes], (8, 128))

    return u[0] * coordinate(0) + u[1] * coordinate(1) + u[2] * coordinate(2), coordinate(3)


def amplitude_kernel(position_ref, point_ref, dir_ref, amp_ref, inten_ref, total_ref):
    group = pl.program_id(0)
    row = rows_of((8, 128))
    lane = lax.broadcasted_iota(jnp.int32, (8, 128), 1)

    u = group_directions(dir_ref, group)
    total = None
    for at in range(LANE_GROUPS // CHUNK):
        left = []
        right = []
        for n in range(CHUNK):
            j = at * CHUNK + n
            turns, weight = group_turns(u, point_ref, j // 2, j % 2)
            powers, step, start = unit_powers(turns)
            high, low = term_rows(powers)
            right.append(jnp.concatenate(high + low, axis=0))
            c, s = weight * start[0], weight * start[1]
            cb, sb = product_conj((c, s), step)
            twice = step[0] + step[0]
            tops = []
            bottoms = []
            for k in range(CENTERS):
                top, bottom = halves(jnp.concatenate([c, s], axis=0))
                tops.append(top)
                bottoms.append(bottom)
                if k + 1 < CENTERS:
                    c, s, cb, sb = twice * c - cb, twice * s - sb, c, s
            left.append(jnp.concatenate(tops + bottoms, axis=0))
        part = lax.dot_general(
            jnp.concatenate(left, axis=1),
            jnp.concatenate(right, axis=1),
            (((1,), (1,)), ((), ())),
            preferred_element_type=F32,
        )
        total = part if total is None else total + part
    total_ref[group] = total[0 : 16 * CENTERS] + total[16 * CENTERS :]

    @pl.when(group == GROUPS - 1)
    def _():
        own = (lane & 7) == row
        front = lane < 8 * SIDE
        squares = [jnp.zeros((8, 128), F32)] * 2
        for g in range(GROUPS):
            real = jnp.zeros((8, 128), F32)
            imag = real
            for k in range(CENTERS):
                c = jnp.sum(jnp.where(own, total_ref[g, 16 * k : 16 * k + 8], 0.0), axis=0, keepdims=True)
                s = jnp.sum(jnp.where(own, total_ref[g, 16 * k + 8 : 16 * k + 16], 0.0), axis=0, keepdims=True)
                real = jnp.where(row == k, c, real)
                imag = jnp.where(row == k, s, imag)
            real = (real + pltpu.roll(real, 64, axis=1)) * NORM
            imag = (imag + pltpu.roll(imag, 64, axis=1)) * NORM
            real_sin = pltpu.roll(real, 96, axis=1)
            imag_sin = pltpu.roll(imag, 96, axis=1)
            planes = [real - imag_sin, real + imag_sin, imag + real_sin, imag - real_sin]
            inside = front & ((lane & 7) + g * 8 < DIR_PART)
            planes = [jnp.where(inside, p, 0.0) for p in planes]
            for i in range(4):
                amp_ref[g, i] = planes[i]
            for i in range(2):
                squares[i] = squares[i] + planes[i] * planes[i] + planes[i + 2] * planes[i + 2]
        spread = jnp.zeros((8, 128), F32)
        for i in range(2):
            square = squares[i]
            for shift in (1, 2, 4):
                square = square + pltpu.roll(square, 128 - shift, axis=1)
            square = jnp.where(front & ((lane & 7) == 0), square, 0.0)
            for k in range(CENTERS):
                spread = spread + pltpu.roll(jnp.where(row == k, square, 0.0), 32 * i + k, axis=1)
        inten_ref[...] = jnp.broadcast_to(jnp.sum(spread, axis=0, keepdims=True), inten_ref.shape)


def point_spec():
    return pl.BlockSpec((PARTS, 4, SOL), lambda g, p: (0, 0, 0))


def direction_spec():
    return pl.BlockSpec((1, 8, 128), lambda g, p: (p[0], 0, 0))


def amplitudes(position, points, directions):
    return pl.pallas_call(
        amplitude_kernel,
        grid_spec=pltpu.PrefetchScalarGridSpec(
            num_scalar_prefetch=1,
            grid=(GROUPS,),
            in_specs=[point_spec(), direction_spec()],
            out_specs=[
                pl.BlockSpec((GROUPS, 4, 8, 128), lambda g, p: (0, 0, 0, 0)),
                pl.BlockSpec((PARTS * REPLICAS, 128), lambda g, p: (0, 0)),
            ],
            scratch_shapes=[pltpu.VMEM((GROUPS, 16 * CENTERS, 128), F32)],
        ),
        out_shape=[
            jax.ShapeDtypeStruct((GROUPS, 4, 8, 128), F32),
            jax.ShapeDtypeStruct((PARTS * REPLICAS, 128), F32),
        ],
        compiler_params=PARAMS,
        cost_estimate=pl.CostEstimate(flops=10_000_000_000, bytes_accessed=1_000_000, transcendentals=0),
        name="amplitudes",
    )(position, points, directions)


def kick_kernel(position_ref, point_ref, dir_ref, amp_ref, inten_ref, shell_ref, out_ref, coef_ref, acc_ref):
    group = pl.program_id(0)
    row = rows_of((8, 128))
    lane = lax.broadcasted_iota(jnp.int32, (8, 128), 1)

    @pl.when(group == 0)
    def _():
        intensity = jnp.sum(inten_ref[...], axis=0, keepdims=True) * (1.0 / (M * REPLICAS))
        at = lax.broadcasted_iota(jnp.int32, (1, 128), 1)
        offset = lax.shift_right_logical(at, 3) & 3
        shell = 8 * (at & 7) + jnp.where((at & 32) == 0, 4 + offset, 3 - offset)
        q = 1.0 + shell.astype(F32) * (3.0 / NQ)
        factor = shell_ref[0:1] * (intensity - shell_ref[1:2]) * (2.0 / M) * q
        scales = []
        for i in range(2):
            scale = jnp.zeros((8, 128), F32)
            for k in range(CENTERS):
                for o in range(SIDE):
                    source = 32 * i + 8 * o + k
                    here = (row == k) & (lax.shift_right_logical(lane, 3) == o)
                    scale = jnp.where(here, jnp.broadcast_to(factor[:, source : source + 1], (8, 128)), scale)
            scales.append(scale)
        acc_ref[...] = jnp.zeros(acc_ref.shape, F32)
        front = lane < 8 * SIDE
        own = (lane & 7) == row
        for g in range(GROUPS):
            b_up = amp_ref[g, 0] * scales[0]
            b_down = amp_ref[g, 1] * scales[1]
            a_up = amp_ref[g, 2] * scales[0]
            a_down = amp_ref[g, 3] * scales[1]
            real = jnp.where(front, a_up + a_down, pltpu.roll(b_down - b_up, 32, axis=1))
            imag = jnp.where(front, b_up + b_down, pltpu.roll(a_up - a_down, 32, axis=1))
            tops = []
            bottoms = []
            for v in (real, imag):
                high = v.astype(BF16).astype(F32)
                tops.append(high + pltpu.roll(high, 64, axis=1))
                bottoms.append(v - high)
            for k in range(CENTERS):
                at = slice(16 * k, 16 * k + 16)
                first = jnp.concatenate([jnp.where(own, v[k : k + 1], 0.0) for v in tops], axis=0).astype(BF16)
                last = jnp.concatenate([jnp.where(own, v[k : k + 1], 0.0) for v in bottoms], axis=0).astype(BF16)
                coef_ref[g, at, 0:128] = first
                coef_ref[g, at, 128:256] = last

    u = group_directions(dir_ref, group)

    for at in range(LANE_GROUPS // CHUNK):
        state = []
        columns = []
        for n in range(CHUNK):
            j = at * CHUNK + n
            turns, _ = group_turns(u, point_ref, j // 2, j % 2)
            powers, step, start = unit_powers(turns)
            high, low = term_rows(powers)
            columns.append(jnp.concatenate(high + low + high, axis=0))
            state.append([step, start, step[0] + step[0]])
        terms = jnp.dot(coef_ref[group, :, 0:192], jnp.concatenate(columns, axis=1), preferred_element_type=F32)
        for n in range(CHUNK):
            step, start, twice = state[n]
            lanes = slice(n * 128, n * 128 + 128)
            r1 = i1 = r2 = i2 = None
            for k in range(CENTERS - 1, -1, -1):
                real = terms[16 * k : 16 * k + 8, lanes]
                imag = terms[16 * k + 8 : 16 * k + 16, lanes]
                if r1 is not None:
                    real = real + twice * r1
                    imag = imag + twice * i1
                if r2 is not None:
                    real = real - r2
                    imag = imag - i2
                r1, i1, r2, i2 = real, imag, r1, i1
            real = r1 - r2 * step[0] - i2 * step[1]
            imag = i1 - i2 * step[0] + r2 * step[1]
            slope = real * start[0] - imag * start[1]
            for c in range(3):
                acc_ref[(at * CHUNK + n) * 3 + c] += u[c] * slope

    @pl.when(group == GROUPS - 1)
    def _():
        for j in range(LANE_GROUPS):
            lanes = slice(j % 2 * 128, j % 2 * 128 + 128)
            for c in range(3):
                out_ref[j // 2, c : c + 1, lanes] = jnp.sum(acc_ref[j * 3 + c], axis=0, keepdims=True) * (1.0 / TURN)


def kicks(position, points, directions, amplitude, intensity, shells):
    return pl.pallas_call(
        kick_kernel,
        grid_spec=pltpu.PrefetchScalarGridSpec(
            num_scalar_prefetch=1,
            grid=(GROUPS,),
            in_specs=[
                point_spec(),
                direction_spec(),
                pl.BlockSpec((GROUPS, 4, 8, 128), lambda g, p: (0, 0, 0, 0)),
                pl.BlockSpec((PARTS * REPLICAS, 128), lambda g, p: (0, 0)),
                pl.BlockSpec((2, 128), lambda g, p: (0, 0)),
            ],
            out_specs=pl.BlockSpec((PARTS, 3, SOL), lambda g, p: (0, 0, 0)),
            scratch_shapes=[
                pltpu.VMEM((GROUPS, 16 * CENTERS, 256), BF16),
                pltpu.VMEM((LANE_GROUPS * 3, 8, 128), F32),
            ],
        ),
        out_shape=jax.ShapeDtypeStruct((PARTS, 3, SOL), F32),
        compiler_params=PARAMS,
        cost_estimate=pl.CostEstimate(flops=10_000_000_000, bytes_accessed=1_000_000, transcendentals=0),
        name="kicks",
    )(position, points, directions, amplitude, intensity, shells)


def exchange(head, tail):
    right = [(i, (i + 1) % PARTS) for i in range(PARTS)]
    left = [((i + 1) % PARTS, i) for i in range(PARTS)]
    return lax.ppermute(tail, "sp", right), lax.ppermute(head, "sp", left)


def to_all(value, axes):
    return lax.all_to_all(value, axes, 0, 0, tiled=True)


def shards(
    positions,
    velocities,
    strength,
    inv_mass,
    tile_lists,
    solute_index,
    scatter_weight,
    intensity_exp,
    precision,
):
    position = lax.axis_index("sp").astype(jnp.int32).reshape(1)
    directions = jnp.asarray(direction_table())
    tiles = tile_lists.reshape(-1)
    shells = jnp.stack([precision, intensity_exp]).reshape(2, CENTERS, 2, SIDE)
    shells = jnp.stack([shells[:, :, 1], shells[:, :, 0, ::-1]], axis=1)
    shells = jnp.pad(jnp.swapaxes(shells, 2, 3), ((0, 0), (0, 2), (0, 0), (0, 8 - CENTERS))).reshape(2, 128)
    state, head, tail, first = pack(
        positions[0], strength, velocities[0], inv_mass, solute_index, scatter_weight
    )
    halo = exchange(head, tail)
    first = to_all(first, "sp")
    state, head, tail = pair_step(0, tiles, position, state, halo)
    halo = exchange(head, tail)
    amp, inten = amplitudes(position, first, directions)
    inten = to_all(inten, ("rep", "sp"))
    state, head, tail, second = pair_step(
        1, tiles, position, state, halo, solute_index, scatter_weight, gathers=True
    )
    halo = exchange(head, tail)
    second = to_all(second, "sp")
    kick = to_all(kicks(position, first, directions, amp, inten, shells), "sp")
    amp, inten = amplitudes(position, second, directions)
    inten = to_all(inten, ("rep", "sp"))
    state, head, tail = pair_step(2, tiles, position, state, halo, solute_index, scatter_weight, kick)
    halo = exchange(head, tail)
    kick = to_all(kicks(position, second, directions, amp, inten, shells), "sp")
    place, speed = pair_step(3, tiles, position, state, halo, last=True)
    speed = finish(speed, inv_mass, solute_index, scatter_weight, kick)
    return (place[None], speed[None])


def solution(mesh):
    in_specs = (
        P("rep", None, "sp"),
        P("rep", None, "sp"),
        P("rep", "sp"),
        P("rep", "sp"),
        P("rep", None, "sp", None),
        P("rep", "sp"),
        P("rep", "sp"),
        P(),
        P(),
    )
    out_specs = (P("rep", None, "sp"), P("rep", None, "sp"))
    return jax.shard_map(shards, mesh=mesh, in_specs=in_specs, out_specs=out_specs, check_vma=False)
```

```python
import functools
import math

import jax
import jax.numpy as jnp
import numpy as np
from jax import lax
from jax.experimental import pallas as pl
from jax.experimental.pallas import tpu as pltpu
from jax.sharding import PartitionSpec as P

M = 784
NQ = 48
OUTER = 2
INNER = 2
TIME_STEP = 0.05
PAIR_STRENGTH = 0.2
HALF_INVERSE = 0.03125

BLOCK = 128
NB = 64
HB = 32
EXT = NB + 2 * HB
NEIGHBOURS = 4
ATOMS = NB * BLOCK
HALO = HB * BLOCK
SOL = 256
PARTS = 8
REPLICAS = 16
DIR_PART = M // PARTS
GROUPS = -(-DIR_PART // 8)
SIDE = 4
CENTERS = NQ // (2 * SIDE)
LANE_GROUPS = PARTS * SOL // 128
CHUNK = 4
FILL_UNROLL = 16
BLOCK_UNROLL = 16

ALPHA = math.sqrt(HALF_INVERSE * math.log2(math.e))
COUPLING = PAIR_STRENGTH / math.sqrt(NEIGHBOURS * BLOCK)
NORM = 1.0 / math.sqrt(PARTS * SOL)
TURN = 1.0 / (64.0 * math.pi)

F32 = jnp.float32
BF16 = jnp.bfloat16


def direction_table():
    order = np.arange(M)
    height = 1.0 - (2.0 * order + 1.0) / M
    radius = np.sqrt(1.0 - height * height)
    azimuth = (order * 610 % 987) * (2.0 * math.pi / 987.0)
    rows = np.stack([radius * np.cos(azimuth), radius * np.sin(azimuth), height], axis=-1) * TURN
    padded = np.zeros((PARTS, GROUPS * 8, 3), np.float32)
    padded[:, :DIR_PART] = rows.reshape(PARTS, DIR_PART, 3)
    table = np.zeros((PARTS, 8, 128), np.float32)
    for c in range(3):
        table[:, :, 16 * c : 16 * c + GROUPS] = np.swapaxes(padded[:, :, c].reshape(PARTS, GROUPS, 8), 1, 2)
    return table


def split3(value):
    high = value.astype(BF16).astype(F32)
    rest = value - high
    mid = rest.astype(BF16).astype(F32)
    return high, mid, rest - mid


def halves(value):
    high = value.astype(BF16)
    return high, (value - high.astype(F32)).astype(BF16)


def rows_of(shape):
    return lax.broadcasted_iota(jnp.int32, shape, 0)


def scaled_parts(cell, factor):
    row = rows_of((8, BLOCK))
    scaled = jnp.concatenate([cell, cell], axis=0) * ALPHA
    norm_row = (row & 3) == 3
    norm = -jnp.sum(jnp.where(row < 3, scaled * scaled, 0.0), axis=0, keepdims=True)
    return split3(jnp.where(norm_row, norm, scaled * factor))


def neighbour_features(cell):
    row = rows_of((8, BLOCK))
    both = jnp.concatenate([cell, cell], axis=0)
    charge = jnp.broadcast_to(cell[3:4], (8, BLOCK))
    moments = jnp.where((row & 3) == 3, charge, both * charge)
    th, tm, tl = split3(moments)
    weights = jnp.concatenate([jnp.where(row < 4, th, tm), jnp.where(row < 4, tl, 0.0)], axis=0)
    h, m, l = scaled_parts(cell, 1.0)
    near = [
        jnp.where((row & 3) == 3, 1.0, jnp.where(row < 4, h, m)),
        jnp.where(row < 3, l, jnp.where(row == 3, 1.0, h)),
        jnp.where(row < 4, m, jnp.where(row < 7, h, l)),
        jnp.zeros((8, BLOCK), F32),
    ]
    return jnp.concatenate(near, axis=0).astype(BF16), weights.astype(BF16)


def own_features(cell):
    row = rows_of((8, BLOCK))
    h, m, l = scaled_parts(cell, 2.0)
    own = [
        jnp.where(row == 7, m, h),
        jnp.where(row < 3, h, jnp.where(row == 3, l, jnp.where(row < 7, m, 1.0))),
        jnp.where((row & 3) == 3, 1.0, jnp.where(row < 4, m, l)),
        jnp.zeros((8, BLOCK), F32),
    ]
    return jnp.concatenate(own, axis=0).astype(BF16)


def selectors(index):
    block = lax.shift_right_logical(index, 7)
    lane = index & 127
    by_block = rows_of((NB, SOL)) == block
    by_lane = rows_of((BLOCK, SOL)) == lane
    return by_block, by_lane


def scatter_kicks(index_ref, weight_ref, kick_ref, push_ref):
    by_block, by_lane = selectors(index_ref[...])
    total = kick_ref[0]
    for part in range(1, PARTS):
        total = total + kick_ref[part]
    total = total * (weight_ref[...] * (-INNER * TIME_STEP))
    lanes = jnp.where(by_lane, 1.0, 0.0).astype(BF16)
    lanes = jnp.concatenate([lanes, lanes, lanes], axis=1)
    for c in range(3):
        parts = split3(total[c : c + 1])
        rows = jnp.concatenate([jnp.where(by_block, p, 0.0).astype(BF16) for p in parts], axis=1)
        push_ref[c] = lax.dot_general(rows, lanes, (((1,), (1,)), ((), ())), preferred_element_type=F32)


def gather_points(index_ref, weight_ref, place_ref, point_ref):
    by_block, by_lane = selectors(index_ref[...])
    lanes = jnp.where(by_lane, 1.0, 0.0).astype(BF16)
    found = []
    for c in range(3):
        total = None
        for p in split3(place_ref[c]):
            part = jnp.dot(p.astype(BF16), lanes, preferred_element_type=F32)
            total = part if total is None else total + part
        found.append(jnp.sum(jnp.where(by_block, total, 0.0), axis=0, keepdims=True))
    found.append(weight_ref[...])
    points = jnp.concatenate(found, axis=0)
    for part in range(PARTS):
        point_ref[part] = points


def block_at(b):
    return pl.ds(pl.multiple_of(b * BLOCK, BLOCK), BLOCK)


def pushed(push_ref, b):
    return jnp.concatenate([push_ref[c, pl.ds(b, 1), :] for c in range(3)], axis=0)


def pack_kernel(pos_ref, charge_ref, vel_ref, inverse_ref, index_ref, weight_ref, *refs):
    out_ref, head_ref, tail_ref, point_ref, place_ref = refs

    def one_block(b, carry):
        at = block_at(b)
        place = pos_ref[:, at]
        out_ref[:, at] = jnp.concatenate([place, charge_ref[:, at], vel_ref[:, at], inverse_ref[:, at]], axis=0)
        for c in range(3):
            place_ref[c, pl.ds(b, 1), :] = place[c : c + 1]
        return carry

    lax.fori_loop(0, NB, one_block, 0, unroll=FILL_UNROLL)
    head_ref[...] = out_ref[0:4, 0:HALO]
    tail_ref[...] = out_ref[0:4, HALO:ATOMS]
    gather_points(index_ref, weight_ref, place_ref, point_ref)


def finish_kernel(vel_ref, inverse_ref, index_ref, weight_ref, kick_ref, out_ref, push_ref):
    scatter_kicks(index_ref, weight_ref, kick_ref, push_ref)

    def one_block(b, carry):
        at = block_at(b)
        out_ref[:, at] = vel_ref[:, at] + inverse_ref[:, at] * pushed(push_ref, b)
        return carry

    lax.fori_loop(0, NB, one_block, 0, unroll=FILL_UNROLL)


def pair_kernel(step, kicked, gathers, last, *refs):
    refs = list(refs)
    fourth_ref, position_ref, state_ref, left_ref, right_ref = refs[:5]
    refs = refs[5:]
    if kicked or gathers:
        index_ref, weight_ref = refs[:2]
        refs = refs[2:]
    if kicked:
        kick_ref = refs.pop(0)
    if last:
        pos_ref, vel_ref = refs[:2]
        refs = refs[2:]
    else:
        out_ref, head_ref, tail_ref = refs[:3]
        refs = refs[3:]
    if gathers:
        point_ref = refs.pop(0)
    near_ref, moment_ref = refs[:2]
    refs = refs[2:]
    if gathers:
        place_ref = refs.pop(0)
    if kicked:
        push_ref = refs.pop(0)

    left_ok = jnp.where(position_ref[0] > 0, 1.0, 0.0)
    right_ok = jnp.where(position_ref[0] < PARTS - 1, 1.0, 0.0)
    row4 = rows_of((4, BLOCK))

    def fill(slot, cell):
        near, moments = neighbour_features(cell)
        near_ref[slot] = near.T
        moment_ref[slot] = moments

    def fill_halo(b, carry):
        at = block_at(b)
        fill(b, left_ref[:, at] * jnp.where(row4 == 3, left_ok, 1.0))
        fill(b + HB + NB, right_ref[:, at] * jnp.where(row4 == 3, right_ok, 1.0))
        return carry

    lax.fori_loop(0, HB, fill_halo, 0, unroll=FILL_UNROLL)

    def fill_own(b, carry):
        cell = state_ref[0:4, block_at(b)]
        fill(b + HB, cell)
        return carry

    lax.fori_loop(0, NB, fill_own, 0, unroll=FILL_UNROLL)

    if kicked:
        scatter_kicks(index_ref, weight_ref, kick_ref, push_ref)

    def update(b, cell, sums):
        sums = sums[0:4] + sums[4:8] + sums[8:12]
        at = block_at(b)
        place, charge, speed, inverse = cell[0:3], cell[3:4], cell[4:7], cell[7:8]
        force = (COUPLING * charge) * (place * sums[3:4] - sums[0:3])
        if kicked:
            speed = speed + inverse * pushed(push_ref, b)
        speed = speed + (TIME_STEP * inverse) * force
        place = place + TIME_STEP * speed
        if gathers:
            for c in range(3):
                place_ref[c, pl.ds(b, 1), :] = place[c : c + 1]
        if last:
            pos_ref[:, at] = place
            vel_ref[:, at] = speed
        else:
            out_ref[:, at] = jnp.concatenate([place, charge, speed, inverse], axis=0)

    def weighted(first, second, own):
        near = jnp.concatenate([near_ref[first], near_ref[second]], axis=0)
        moments = jnp.concatenate([moment_ref[first], moment_ref[second]], axis=1)
        high, low = halves(jnp.exp2(jnp.dot(near, own, preferred_element_type=F32)))
        sums = jnp.dot(moments, high, preferred_element_type=F32)
        return sums + jnp.dot(moments, low, preferred_element_type=F32)

    def one_pair(b, carry):
        c = b + HB
        cells = [state_ref[:, block_at(b)], state_ref[:, block_at(c)]]
        own = [own_features(v[0:4]) for v in cells]
        shared = weighted(b + HB, b + 2 * HB, jnp.concatenate(own, axis=1))
        left = weighted(b, fourth_ref[step * NB + b], own[0])
        right = weighted(b + 3 * HB, fourth_ref[step * NB + c], own[1])
        update(b, cells[0], shared[:, 0:BLOCK] + left)
        update(c, cells[1], shared[:, BLOCK:] + right)
        return carry

    lax.fori_loop(0, HB, one_pair, 0, unroll=BLOCK_UNROLL)

    if not last:
        head_ref[...] = out_ref[0:4, 0:HALO]
        tail_ref[...] = out_ref[0:4, HALO:ATOMS]
    if gathers:
        gather_points(index_ref, weight_ref, place_ref, point_ref)


VMEM = pl.BlockSpec(memory_space=pltpu.VMEM)
SMEM = pl.BlockSpec(memory_space=pltpu.SMEM)
PARAMS = pltpu.CompilerParams(vmem_limit_bytes=32 << 20)


def pack(positions, strength, velocities, inv_mass, index, weights):
    return pl.pallas_call(
        pack_kernel,
        out_shape=[
            jax.ShapeDtypeStruct((8, ATOMS), F32),
            jax.ShapeDtypeStruct((4, HALO), F32),
            jax.ShapeDtypeStruct((4, HALO), F32),
            jax.ShapeDtypeStruct((PARTS, 4, SOL), F32),
        ],
        in_specs=[VMEM] * 6,
        out_specs=[VMEM] * 4,
        scratch_shapes=[pltpu.VMEM((3, NB, BLOCK), F32)],
        compiler_params=PARAMS,
        cost_estimate=pl.CostEstimate(flops=100_000_000, bytes_accessed=600_000, transcendentals=0),
        name="pack",
    )(positions, strength, velocities, inv_mass, index, weights)


def finish(velocities, inv_mass, index, weights, kick):
    return pl.pallas_call(
        finish_kernel,
        out_shape=jax.ShapeDtypeStruct((3, ATOMS), F32),
        in_specs=[VMEM] * 5,
        out_specs=VMEM,
        scratch_shapes=[pltpu.VMEM((3, NB, BLOCK), F32)],
        compiler_params=PARAMS,
        cost_estimate=pl.CostEstimate(flops=100_000_000, bytes_accessed=300_000, transcendentals=0),
        name="finish",
    )(velocities, inv_mass, index, weights, kick)


def pair_step(step, tiles, position, state, halo, index=None, weights=None, kick=None, gathers=False, last=False):
    kicked = kick is not None
    operands = [tiles, position, state, halo[0], halo[1]]
    specs = [SMEM, SMEM, VMEM, VMEM, VMEM]
    if kicked or gathers:
        operands += [index, weights]
        specs += [VMEM, VMEM]
    if kicked:
        operands.append(kick)
        specs.append(VMEM)
    scratch = [
        pltpu.VMEM((EXT, BLOCK, 32), BF16),
        pltpu.VMEM((EXT, 16, BLOCK), BF16),
    ]
    if last:
        shapes = [jax.ShapeDtypeStruct((3, ATOMS), F32)] * 2
    else:
        shapes = [jax.ShapeDtypeStruct((8, ATOMS), F32)] + [jax.ShapeDtypeStruct((4, HALO), F32)] * 2
    if gathers:
        shapes.append(jax.ShapeDtypeStruct((PARTS, 4, SOL), F32))
        scratch.append(pltpu.VMEM((3, NB, BLOCK), F32))
    if kicked:
        scratch.append(pltpu.VMEM((3, NB, BLOCK), F32))
    return pl.pallas_call(
        functools.partial(pair_kernel, step, kicked, gathers, last),
        out_shape=shapes,
        in_specs=specs,
        out_specs=[VMEM] * len(shapes),
        scratch_shapes=scratch,
        compiler_params=PARAMS,
        cost_estimate=pl.CostEstimate(flops=6_000_000_000, bytes_accessed=2_000_000, transcendentals=4_000_000),
        name="pair_step",
    )(*operands)


def double(cos, sin):
    twice = sin + sin
    return 1.0 - twice * sin, twice * cos


def product(a, b):
    return a[0] * b[0] - a[1] * b[1], a[1] * b[0] + a[0] * b[1]


def product_conj(a, b):
    return a[0] * b[0] + a[1] * b[1], a[1] * b[0] - a[0] * b[1]


def unit_powers(turns):
    y = (turns - jnp.round(turns)) * (0.5 * math.pi)
    z = y * y
    sin = ((-1.9515295891e-4 * z + 8.3321608736e-3) * z - 1.6666654611e-1) * (z * y) + y
    cos = ((2.443315711809948e-5 * z - 1.388731625493765e-3) * z + 4.166664568298827e-2) * (z * z) + (1.0 - 0.5 * z)
    one = double(*double(cos, sin))
    two = double(*one)
    three = product(two, one)
    five = product(three, two)
    seven = product(five, two)
    sixteen = double(*double(*double(*two)))
    return [one, three, five, seven], sixteen, product(double(*sixteen), seven)


def term_rows(powers):
    values = [p[0] for p in powers] + [p[1] for p in powers]
    parts = [halves(jnp.concatenate(values[i : i + 2], axis=0)) for i in range(0, 8, 2)]
    return [p[0] for p in parts], [p[1] for p in parts]


def group_directions(dir_ref, group):
    return [jnp.broadcast_to(dir_ref[0, :, 16 * c + group : 16 * c + group + 1], (8, 128)) for c in range(3)]


def group_turns(u, point_ref, part, half):
    lanes = slice(half * 128, half * 128 + 128)

    def coordinate(c):
        return jnp.broadcast_to(point_ref[part, c : c + 1, lanes], (8, 128))

    return u[0] * coordinate(0) + u[1] * coordinate(1) + u[2] * coordinate(2), coordinate(3)


def amplitude_kernel(position_ref, point_ref, dir_ref, amp_ref, inten_ref, total_ref):
    row = rows_of((8, 128))
    lane = lax.broadcasted_iota(jnp.int32, (8, 128), 1)

    for group in range(GROUPS):
        u = group_directions(dir_ref, group)
        total = None
        for at in range(LANE_GROUPS // CHUNK):
            left = []
            right = []
            for n in range(CHUNK):
                j = at * CHUNK + n
                turns, weight = group_turns(u, point_ref, j // 2, j % 2)
                powers, step, start = unit_powers(turns)
                high, low = term_rows(powers)
                right.append(jnp.concatenate(high + low, axis=0))
                c, s = weight * start[0], weight * start[1]
                cb, sb = product_conj((c, s), step)
                twice = step[0] + step[0]
                tops = []
                bottoms = []
                for k in range(CENTERS):
                    top, bottom = halves(jnp.concatenate([c, s], axis=0))
                    tops.append(top)
                    bottoms.append(bottom)
                    if k + 1 < CENTERS:
                        c, s, cb, sb = twice * c - cb, twice * s - sb, c, s
                left.append(jnp.concatenate(tops + bottoms, axis=0))
            part = lax.dot_general(
                jnp.concatenate(left, axis=1),
                jnp.concatenate(right, axis=1),
                (((1,), (1,)), ((), ())),
                preferred_element_type=F32,
            )
            total = part if total is None else total + part
        total_ref[group] = total[0 : 16 * CENTERS] + total[16 * CENTERS :]

    own = (lane & 7) == row
    front = lane < 8 * SIDE
    squares = [jnp.zeros((8, 128), F32)] * 2
    for g in range(GROUPS):
        real = jnp.zeros((8, 128), F32)
        imag = real
        for k in range(CENTERS):
            c = jnp.sum(jnp.where(own, total_ref[g, 16 * k : 16 * k + 8], 0.0), axis=0, keepdims=True)
            s = jnp.sum(jnp.where(own, total_ref[g, 16 * k + 8 : 16 * k + 16], 0.0), axis=0, keepdims=True)
            real = jnp.where(row == k, c, real)
            imag = jnp.where(row == k, s, imag)
        real = (real + pltpu.roll(real, 64, axis=1)) * NORM
        imag = (imag + pltpu.roll(imag, 64, axis=1)) * NORM
        real_sin = pltpu.roll(real, 96, axis=1)
        imag_sin = pltpu.roll(imag, 96, axis=1)
        planes = [real - imag_sin, real + imag_sin, imag + real_sin, imag - real_sin]
        inside = front & ((lane & 7) + g * 8 < DIR_PART)
        planes = [jnp.where(inside, p, 0.0) for p in planes]
        for i in range(4):
            amp_ref[g, i] = planes[i]
        for i in range(2):
            squares[i] = squares[i] + planes[i] * planes[i] + planes[i + 2] * planes[i + 2]
    spread = jnp.zeros((8, 128), F32)
    for i in range(2):
        square = squares[i]
        for shift in (1, 2, 4):
            square = square + pltpu.roll(square, 128 - shift, axis=1)
        square = jnp.where(front & ((lane & 7) == 0), square, 0.0)
        for k in range(CENTERS):
            spread = spread + pltpu.roll(jnp.where(row == k, square, 0.0), 32 * i + k, axis=1)
    inten_ref[...] = jnp.broadcast_to(jnp.sum(spread, axis=0, keepdims=True), inten_ref.shape)


def point_spec():
    return pl.BlockSpec((PARTS, 4, SOL), lambda g, p: (0, 0, 0))


def direction_spec():
    return pl.BlockSpec((1, 8, 128), lambda g, p: (p[0], 0, 0))


def amplitudes(position, points, directions):
    return pl.pallas_call(
        amplitude_kernel,
        grid_spec=pltpu.PrefetchScalarGridSpec(
            num_scalar_prefetch=1,
            grid=(1,),
            in_specs=[point_spec(), direction_spec()],
            out_specs=[
                pl.BlockSpec((GROUPS, 4, 8, 128), lambda g, p: (0, 0, 0, 0)),
                pl.BlockSpec((PARTS * REPLICAS, 128), lambda g, p: (0, 0)),
            ],
            scratch_shapes=[pltpu.VMEM((GROUPS, 16 * CENTERS, 128), F32)],
        ),
        out_shape=[
            jax.ShapeDtypeStruct((GROUPS, 4, 8, 128), F32),
            jax.ShapeDtypeStruct((PARTS * REPLICAS, 128), F32),
        ],
        compiler_params=PARAMS,
        cost_estimate=pl.CostEstimate(flops=10_000_000_000, bytes_accessed=1_000_000, transcendentals=0),
        name="amplitudes",
    )(position, points, directions)


def kick_kernel(position_ref, point_ref, dir_ref, amp_ref, inten_ref, shell_ref, out_ref, coef_ref):
    row = rows_of((8, 128))
    lane = lax.broadcasted_iota(jnp.int32, (8, 128), 1)

    intensity = jnp.sum(inten_ref[...], axis=0, keepdims=True) * (1.0 / (M * REPLICAS))
    at = lax.broadcasted_iota(jnp.int32, (1, 128), 1)
    offset = lax.shift_right_logical(at, 3) & 3
    shell = 8 * (at & 7) + jnp.where((at & 32) == 0, 4 + offset, 3 - offset)
    q = 1.0 + shell.astype(F32) * (3.0 / NQ)
    factor = shell_ref[0:1] * (intensity - shell_ref[1:2]) * (2.0 / M) * q
    scales = []
    for i in range(2):
        scale = jnp.zeros((8, 128), F32)
        for k in range(CENTERS):
            for o in range(SIDE):
                source = 32 * i + 8 * o + k
                here = (row == k) & (lax.shift_right_logical(lane, 3) == o)
                scale = jnp.where(here, jnp.broadcast_to(factor[:, source : source + 1], (8, 128)), scale)
        scales.append(scale)
    kicked = [[None] * 3 for _ in range(LANE_GROUPS)]
    front = lane < 8 * SIDE
    own = (lane & 7) == row
    for g in range(GROUPS):
        b_up = amp_ref[g, 0] * scales[0]
        b_down = amp_ref[g, 1] * scales[1]
        a_up = amp_ref[g, 2] * scales[0]
        a_down = amp_ref[g, 3] * scales[1]
        real = jnp.where(front, a_up + a_down, pltpu.roll(b_down - b_up, 32, axis=1))
        imag = jnp.where(front, b_up + b_down, pltpu.roll(a_up - a_down, 32, axis=1))
        tops = []
        bottoms = []
        for v in (real, imag):
            high = v.astype(BF16).astype(F32)
            tops.append(high + pltpu.roll(high, 64, axis=1))
            bottoms.append(v - high)
        for k in range(CENTERS):
            at = slice(16 * k, 16 * k + 16)
            first = jnp.concatenate([jnp.where(own, v[k : k + 1], 0.0) for v in tops], axis=0).astype(BF16)
            last = jnp.concatenate([jnp.where(own, v[k : k + 1], 0.0) for v in bottoms], axis=0).astype(BF16)
            coef_ref[g, at, 0:128] = first
            coef_ref[g, at, 128:256] = last

    for group in range(GROUPS):
        u = group_directions(dir_ref, group)

        for at in range(LANE_GROUPS // CHUNK):
            state = []
            columns = []
            for n in range(CHUNK):
                j = at * CHUNK + n
                turns, _ = group_turns(u, point_ref, j // 2, j % 2)
                powers, step, start = unit_powers(turns)
                high, low = term_rows(powers)
                columns.append(jnp.concatenate(high + low + high, axis=0))
                state.append([step, start, step[0] + step[0]])
            terms = jnp.dot(coef_ref[group, :, 0:192], jnp.concatenate(columns, axis=1), preferred_element_type=F32)
            for n in range(CHUNK):
                step, start, twice = state[n]
                lanes = slice(n * 128, n * 128 + 128)
                r1 = i1 = r2 = i2 = None
                for k in range(CENTERS - 1, -1, -1):
                    real = terms[16 * k : 16 * k + 8, lanes]
                    imag = terms[16 * k + 8 : 16 * k + 16, lanes]
                    if r1 is not None:
                        real = real + twice * r1
                        imag = imag + twice * i1
                    if r2 is not None:
                        real = real - r2
                        imag = imag - i2
                    r1, i1, r2, i2 = real, imag, r1, i1
                real = r1 - r2 * step[0] - i2 * step[1]
                imag = i1 - i2 * step[0] + r2 * step[1]
                slope = real * start[0] - imag * start[1]
                for c in range(3):
                    value = u[c] * slope
                    old = kicked[at * CHUNK + n][c]
                    kicked[at * CHUNK + n][c] = value if old is None else old + value

    for j in range(LANE_GROUPS):
        lanes = slice(j % 2 * 128, j % 2 * 128 + 128)
        for c in range(3):
            out_ref[j // 2, c : c + 1, lanes] = jnp.sum(kicked[j][c], axis=0, keepdims=True) * (1.0 / TURN)


def kicks(position, points, directions, amplitude, intensity, shells):
    return pl.pallas_call(
        kick_kernel,
        grid_spec=pltpu.PrefetchScalarGridSpec(
            num_scalar_prefetch=1,
            grid=(1,),
            in_specs=[
                point_spec(),
                direction_spec(),
                pl.BlockSpec((GROUPS, 4, 8, 128), lambda g, p: (0, 0, 0, 0)),
                pl.BlockSpec((PARTS * REPLICAS, 128), lambda g, p: (0, 0)),
                pl.BlockSpec((2, 128), lambda g, p: (0, 0)),
            ],
            out_specs=pl.BlockSpec((PARTS, 3, SOL), lambda g, p: (0, 0, 0)),
            scratch_shapes=[
                pltpu.VMEM((GROUPS, 16 * CENTERS, 256), BF16),
            ],
        ),
        out_shape=jax.ShapeDtypeStruct((PARTS, 3, SOL), F32),
        compiler_params=PARAMS,
        cost_estimate=pl.CostEstimate(flops=10_000_000_000, bytes_accessed=1_000_000, transcendentals=0),
        name="kicks",
    )(position, points, directions, amplitude, intensity, shells)


def exchange(head, tail):
    right = [(i, (i + 1) % PARTS) for i in range(PARTS)]
    left = [((i + 1) % PARTS, i) for i in range(PARTS)]
    return lax.ppermute(tail, "sp", right), lax.ppermute(head, "sp", left)


def to_all(value, axes):
    return lax.all_to_all(value, axes, 0, 0, tiled=True)


def shards(
    positions,
    velocities,
    strength,
    inv_mass,
    tile_lists,
    solute_index,
    scatter_weight,
    intensity_exp,
    precision,
):
    position = lax.axis_index("sp").astype(jnp.int32).reshape(1)
    directions = jnp.asarray(direction_table())
    usual = 3 * (jnp.arange(NB, dtype=jnp.int32) + HB)
    tiles = (jnp.sum(tile_lists[0], axis=-1) - usual).reshape(-1)
    shells = jnp.stack([precision, intensity_exp]).reshape(2, CENTERS, 2, SIDE)
    shells = jnp.stack([shells[:, :, 1], shells[:, :, 0, ::-1]], axis=1)
    shells = jnp.pad(jnp.swapaxes(shells, 2, 3), ((0, 0), (0, 2), (0, 0), (0, 8 - CENTERS))).reshape(2, 128)
    state, head, tail, first = pack(
        positions[0], strength, velocities[0], inv_mass, solute_index, scatter_weight
    )
    halo = exchange(head, tail)
    first = to_all(first, "sp")
    state, head, tail = pair_step(0, tiles, position, state, halo)
    halo = exchange(head, tail)
    amp, inten = amplitudes(position, first, directions)
    inten = to_all(inten, ("rep", "sp"))
    state, head, tail, second = pair_step(
        1, tiles, position, state, halo, solute_index, scatter_weight, gathers=True
    )
    halo = exchange(head, tail)
    second = to_all(second, "sp")
    kick = to_all(kicks(position, first, directions, amp, inten, shells), "sp")
    amp, inten = amplitudes(position, second, directions)
    inten = to_all(inten, ("rep", "sp"))
    state, head, tail = pair_step(2, tiles, position, state, halo, solute_index, scatter_weight, kick)
    halo = exchange(head, tail)
    kick = to_all(kicks(position, second, directions, amp, inten, shells), "sp")
    place, speed = pair_step(3, tiles, position, state, halo, last=True)
    speed = finish(speed, inv_mass, solute_index, scatter_weight, kick)
    return (place[None], speed[None])


def solution(mesh):
    in_specs = (
        P("rep", None, "sp"),
        P("rep", None, "sp"),
        P("rep", "sp"),
        P("rep", "sp"),
        P("rep", None, "sp", None),
        P("rep", "sp"),
        P("rep", "sp"),
        P(),
        P(),
    )
    out_specs = (P("rep", None, "sp"), P("rep", None, "sp"))
    return jax.shard_map(shards, mesh=mesh, in_specs=in_specs, out_specs=out_specs, check_vma=False)
```

```python
import functools
import math

import jax
import jax.numpy as jnp
import numpy as np
from jax import lax
from jax.experimental import pallas as pl
from jax.experimental.pallas import tpu as pltpu
from jax.sharding import PartitionSpec as P

M = 784
NQ = 48
OUTER = 2
INNER = 2
TIME_STEP = 0.05
PAIR_STRENGTH = 0.2
HALF_INVERSE = 0.03125

BLOCK = 128
NB = 64
HB = 32
EXT = NB + 2 * HB
NEIGHBOURS = 4
ATOMS = NB * BLOCK
HALO = HB * BLOCK
SOL = 256
PARTS = 8
REPLICAS = 16
DIR_PART = M // PARTS
STEP_GROUPS = 7
STEPS = 2
GROUPS = STEPS * STEP_GROUPS
SIDE = 4
CENTERS = NQ // (2 * SIDE)
LANE_GROUPS = PARTS * SOL // 128
CHUNK = 4
FILL_UNROLL = 32
BLOCK_UNROLL = 16

ALPHA = math.sqrt(HALF_INVERSE * math.log2(math.e))
COUPLING = PAIR_STRENGTH / math.sqrt(NEIGHBOURS * BLOCK)
NORM = 1.0 / math.sqrt(PARTS * SOL)
TURN = 1.0 / (64.0 * math.pi)

F32 = jnp.float32
BF16 = jnp.bfloat16


def direction_table():
    order = np.arange(M)
    height = 1.0 - (2.0 * order + 1.0) / M
    radius = np.sqrt(1.0 - height * height)
    azimuth = (order * 610 % 987) * (2.0 * math.pi / 987.0)
    rows = np.stack([radius * np.cos(azimuth), radius * np.sin(azimuth), height], axis=-1) * TURN
    padded = np.zeros((PARTS, GROUPS * 8, 3), np.float32)
    padded[:, :DIR_PART] = rows.reshape(PARTS, DIR_PART, 3)
    table = np.zeros((PARTS, STEPS, 8, 128), np.float32)
    for c in range(3):
        part = padded[:, :, c].reshape(PARTS, STEPS, STEP_GROUPS, 8)
        table[:, :, :, 16 * c : 16 * c + STEP_GROUPS] = np.swapaxes(part, 2, 3)
    return table


def split3(value):
    high = value.astype(BF16).astype(F32)
    rest = value - high
    mid = rest.astype(BF16).astype(F32)
    return high, mid, rest - mid


def halves(value):
    high = value.astype(BF16)
    return high, (value - high.astype(F32)).astype(BF16)


def rows_of(shape):
    return lax.broadcasted_iota(jnp.int32, shape, 0)


def scaled_parts(cell, factor):
    row = rows_of((8, BLOCK))
    scaled = jnp.concatenate([cell, cell], axis=0) * ALPHA
    norm_row = (row & 3) == 3
    norm = -jnp.sum(jnp.where(row < 3, scaled * scaled, 0.0), axis=0, keepdims=True)
    return split3(jnp.where(norm_row, norm, scaled * factor))


def neighbour_features(cell):
    row = rows_of((8, BLOCK))
    both = jnp.concatenate([cell, cell], axis=0)
    charge = jnp.broadcast_to(cell[3:4], (8, BLOCK))
    moments = jnp.where((row & 3) == 3, charge, both * charge)
    th, tm, tl = split3(moments)
    weights = jnp.concatenate([jnp.where(row < 4, th, tm), jnp.where(row < 4, tl, 0.0)], axis=0)
    h, m, l = scaled_parts(cell, 1.0)
    near = [
        jnp.where((row & 3) == 3, 1.0, jnp.where(row < 4, h, m)),
        jnp.where(row < 3, l, jnp.where(row == 3, 1.0, h)),
        jnp.where(row < 4, m, jnp.where(row < 7, h, l)),
        jnp.zeros((8, BLOCK), F32),
    ]
    return jnp.concatenate(near, axis=0).astype(BF16), weights.astype(BF16)


def own_features(cell):
    row = rows_of((8, BLOCK))
    h, m, l = scaled_parts(cell, 2.0)
    own = [
        jnp.where(row == 7, m, h),
        jnp.where(row < 3, h, jnp.where(row == 3, l, jnp.where(row < 7, m, 1.0))),
        jnp.where((row & 3) == 3, 1.0, jnp.where(row < 4, m, l)),
        jnp.zeros((8, BLOCK), F32),
    ]
    return jnp.concatenate(own, axis=0).astype(BF16)


def selectors(index):
    block = lax.shift_right_logical(index, 7)
    lane = index & 127
    by_block = rows_of((NB, SOL)) == block
    by_lane = rows_of((BLOCK, SOL)) == lane
    return by_block, by_lane


def scatter_kicks(index_ref, weight_ref, kick_ref, push_ref):
    by_block, by_lane = selectors(index_ref[...])
    total = kick_ref[0]
    for part in range(1, PARTS):
        total = total + kick_ref[part]
    total = total * (weight_ref[...] * (-INNER * TIME_STEP))
    lanes = jnp.where(by_lane, 1.0, 0.0).astype(BF16)
    lanes = jnp.concatenate([lanes, lanes, lanes], axis=1)
    for c in range(3):
        parts = split3(total[c : c + 1])
        rows = jnp.concatenate([jnp.where(by_block, p, 0.0).astype(BF16) for p in parts], axis=1)
        push_ref[c] = lax.dot_general(rows, lanes, (((1,), (1,)), ((), ())), preferred_element_type=F32)


def gather_points(index_ref, weight_ref, place_ref, point_ref):
    by_block, by_lane = selectors(index_ref[...])
    lanes = jnp.where(by_lane, 1.0, 0.0).astype(BF16)
    found = []
    for c in range(3):
        total = None
        for p in split3(place_ref[c]):
            part = jnp.dot(p.astype(BF16), lanes, preferred_element_type=F32)
            total = part if total is None else total + part
        found.append(jnp.sum(jnp.where(by_block, total, 0.0), axis=0, keepdims=True))
    found.append(weight_ref[...])
    points = jnp.concatenate(found, axis=0)
    for part in range(PARTS):
        point_ref[part] = points


def block_at(b):
    return pl.ds(pl.multiple_of(b * BLOCK, BLOCK), BLOCK)


def pushed(push_ref, b):
    return jnp.concatenate([push_ref[c, pl.ds(b, 1), :] for c in range(3)], axis=0)


def pack_kernel(pos_ref, charge_ref, vel_ref, inverse_ref, index_ref, weight_ref, *refs):
    out_ref, head_ref, tail_ref, point_ref, place_ref = refs

    def one_block(b, carry):
        at = block_at(b)
        place = pos_ref[:, at]
        out_ref[:, at] = jnp.concatenate([place, charge_ref[:, at], vel_ref[:, at], inverse_ref[:, at]], axis=0)
        for c in range(3):
            place_ref[c, pl.ds(b, 1), :] = place[c : c + 1]
        return carry

    lax.fori_loop(0, NB, one_block, 0, unroll=FILL_UNROLL)
    head_ref[...] = out_ref[0:4, 0:HALO]
    tail_ref[...] = out_ref[0:4, HALO:ATOMS]
    gather_points(index_ref, weight_ref, place_ref, point_ref)


def finish_kernel(vel_ref, inverse_ref, index_ref, weight_ref, kick_ref, out_ref, push_ref):
    scatter_kicks(index_ref, weight_ref, kick_ref, push_ref)

    def one_block(b, carry):
        at = block_at(b)
        out_ref[:, at] = vel_ref[:, at] + inverse_ref[:, at] * pushed(push_ref, b)
        return carry

    lax.fori_loop(0, NB, one_block, 0, unroll=FILL_UNROLL)


def pair_kernel(step, kicked, gathers, last, *refs):
    refs = list(refs)
    fourth_ref, position_ref, state_ref, left_ref, right_ref = refs[:5]
    refs = refs[5:]
    if kicked or gathers:
        index_ref, weight_ref = refs[:2]
        refs = refs[2:]
    if kicked:
        kick_ref = refs.pop(0)
    if last:
        pos_ref, vel_ref = refs[:2]
        refs = refs[2:]
    else:
        out_ref, head_ref, tail_ref = refs[:3]
        refs = refs[3:]
    if gathers:
        point_ref = refs.pop(0)
    near_ref, moment_ref = refs[:2]
    refs = refs[2:]
    if gathers:
        place_ref = refs.pop(0)
    if kicked:
        push_ref = refs.pop(0)

    left_ok = jnp.where(position_ref[0] > 0, 1.0, 0.0)
    right_ok = jnp.where(position_ref[0] < PARTS - 1, 1.0, 0.0)
    row4 = rows_of((4, BLOCK))

    def fill(slot, cell):
        near, moments = neighbour_features(cell)
        near_ref[slot] = near.T
        moment_ref[slot] = moments

    def fill_halo(b, carry):
        at = block_at(b)
        fill(b, left_ref[:, at] * jnp.where(row4 == 3, left_ok, 1.0))
        fill(b + HB + NB, right_ref[:, at] * jnp.where(row4 == 3, right_ok, 1.0))
        return carry

    lax.fori_loop(0, HB, fill_halo, 0, unroll=FILL_UNROLL)

    def fill_own(b, carry):
        cell = state_ref[0:4, block_at(b)]
        fill(b + HB, cell)
        return carry

    lax.fori_loop(0, NB, fill_own, 0, unroll=FILL_UNROLL)

    if kicked:
        scatter_kicks(index_ref, weight_ref, kick_ref, push_ref)

    def update(b, cell, sums):
        sums = sums[0:4] + sums[4:8] + sums[8:12]
        at = block_at(b)
        place, charge, speed, inverse = cell[0:3], cell[3:4], cell[4:7], cell[7:8]
        force = (COUPLING * charge) * (place * sums[3:4] - sums[0:3])
        if kicked:
            speed = speed + inverse * pushed(push_ref, b)
        speed = speed + (TIME_STEP * inverse) * force
        place = place + TIME_STEP * speed
        if gathers:
            for c in range(3):
                place_ref[c, pl.ds(b, 1), :] = place[c : c + 1]
        if last:
            pos_ref[:, at] = place
            vel_ref[:, at] = speed
        else:
            out_ref[:, at] = jnp.concatenate([place, charge, speed, inverse], axis=0)

    def weighted(first, second, own):
        near = jnp.concatenate([near_ref[first], near_ref[second]], axis=0)
        moments = jnp.concatenate([moment_ref[first], moment_ref[second]], axis=1)
        high, low = halves(jnp.exp2(jnp.dot(near, own, preferred_element_type=F32)))
        sums = jnp.dot(moments, high, preferred_element_type=F32)
        return sums + jnp.dot(moments, low, preferred_element_type=F32)

    def one_pair(b, carry):
        c = b + HB
        cells = [state_ref[:, block_at(b)], state_ref[:, block_at(c)]]
        own = [own_features(v[0:4]) for v in cells]
        shared = weighted(b + HB, b + 2 * HB, jnp.concatenate(own, axis=1))
        left = weighted(b, fourth_ref[step * NB + b], own[0])
        right = weighted(b + 3 * HB, fourth_ref[step * NB + c], own[1])
        update(b, cells[0], shared[:, 0:BLOCK] + left)
        update(c, cells[1], shared[:, BLOCK:] + right)
        return carry

    lax.fori_loop(0, HB, one_pair, 0, unroll=BLOCK_UNROLL)

    if not last:
        head_ref[...] = out_ref[0:4, 0:HALO]
        tail_ref[...] = out_ref[0:4, HALO:ATOMS]
    if gathers:
        gather_points(index_ref, weight_ref, place_ref, point_ref)


VMEM = pl.BlockSpec(memory_space=pltpu.VMEM)
SMEM = pl.BlockSpec(memory_space=pltpu.SMEM)
PARAMS = pltpu.CompilerParams(vmem_limit_bytes=32 << 20)


def pack(positions, strength, velocities, inv_mass, index, weights):
    return pl.pallas_call(
        pack_kernel,
        out_shape=[
            jax.ShapeDtypeStruct((8, ATOMS), F32),
            jax.ShapeDtypeStruct((4, HALO), F32),
            jax.ShapeDtypeStruct((4, HALO), F32),
            jax.ShapeDtypeStruct((PARTS, 4, SOL), F32),
        ],
        in_specs=[VMEM] * 6,
        out_specs=[VMEM] * 4,
        scratch_shapes=[pltpu.VMEM((3, NB, BLOCK), F32)],
        compiler_params=PARAMS,
        cost_estimate=pl.CostEstimate(flops=100_000_000, bytes_accessed=600_000, transcendentals=0),
        name="pack",
    )(positions, strength, velocities, inv_mass, index, weights)


def finish(velocities, inv_mass, index, weights, kick):
    return pl.pallas_call(
        finish_kernel,
        out_shape=jax.ShapeDtypeStruct((3, ATOMS), F32),
        in_specs=[VMEM] * 5,
        out_specs=VMEM,
        scratch_shapes=[pltpu.VMEM((3, NB, BLOCK), F32)],
        compiler_params=PARAMS,
        cost_estimate=pl.CostEstimate(flops=100_000_000, bytes_accessed=300_000, transcendentals=0),
        name="finish",
    )(velocities, inv_mass, index, weights, kick)


def pair_step(step, tiles, position, state, halo, index=None, weights=None, kick=None, gathers=False, last=False):
    kicked = kick is not None
    operands = [tiles, position, state, halo[0], halo[1]]
    specs = [SMEM, SMEM, VMEM, VMEM, VMEM]
    if kicked or gathers:
        operands += [index, weights]
        specs += [VMEM, VMEM]
    if kicked:
        operands.append(kick)
        specs.append(VMEM)
    scratch = [
        pltpu.VMEM((EXT, BLOCK, 32), BF16),
        pltpu.VMEM((EXT, 16, BLOCK), BF16),
    ]
    if last:
        shapes = [jax.ShapeDtypeStruct((3, ATOMS), F32)] * 2
    else:
        shapes = [jax.ShapeDtypeStruct((8, ATOMS), F32)] + [jax.ShapeDtypeStruct((4, HALO), F32)] * 2
    if gathers:
        shapes.append(jax.ShapeDtypeStruct((PARTS, 4, SOL), F32))
        scratch.append(pltpu.VMEM((3, NB, BLOCK), F32))
    if kicked:
        scratch.append(pltpu.VMEM((3, NB, BLOCK), F32))
    return pl.pallas_call(
        functools.partial(pair_kernel, step, kicked, gathers, last),
        out_shape=shapes,
        in_specs=specs,
        out_specs=[VMEM] * len(shapes),
        scratch_shapes=scratch,
        compiler_params=PARAMS,
        cost_estimate=pl.CostEstimate(flops=6_000_000_000, bytes_accessed=2_000_000, transcendentals=4_000_000),
        name="pair_step",
    )(*operands)


def double(cos, sin):
    twice = sin + sin
    return 1.0 - twice * sin, twice * cos


def product(a, b):
    return a[0] * b[0] - a[1] * b[1], a[1] * b[0] + a[0] * b[1]


def product_conj(a, b):
    return a[0] * b[0] + a[1] * b[1], a[1] * b[0] - a[0] * b[1]


def unit_powers(turns):
    y = (turns - jnp.round(turns)) * (0.5 * math.pi)
    z = y * y
    sin = ((-1.9515295891e-4 * z + 8.3321608736e-3) * z - 1.6666654611e-1) * (z * y) + y
    cos = ((2.443315711809948e-5 * z - 1.388731625493765e-3) * z + 4.166664568298827e-2) * (z * z) + (1.0 - 0.5 * z)
    one = double(*double(cos, sin))
    two = double(*one)
    three = product(two, one)
    five = product(three, two)
    seven = product(five, two)
    sixteen = double(*double(*double(*two)))
    return [one, three, five, seven], sixteen, product(double(*sixteen), seven)


def term_rows(powers):
    values = [p[0] for p in powers] + [p[1] for p in powers]
    parts = [halves(jnp.concatenate(values[i : i + 2], axis=0)) for i in range(0, 8, 2)]
    return [p[0] for p in parts], [p[1] for p in parts]


def group_directions(dir_ref, group):
    return [jnp.broadcast_to(dir_ref[0, 0, :, 16 * c + group : 16 * c + group + 1], (8, 128)) for c in range(3)]


def group_turns(u, point_ref, part, half):
    lanes = slice(half * 128, half * 128 + 128)

    def coordinate(c):
        return jnp.broadcast_to(point_ref[part, c : c + 1, lanes], (8, 128))

    return u[0] * coordinate(0) + u[1] * coordinate(1) + u[2] * coordinate(2), coordinate(3)


def shell_of(down, k, o):
    return 8 * k + 3 - o if down else 8 * k + 4 + o


def amplitude_kernel(position_ref, point_ref, dir_ref, amp_ref, inten_ref, total_ref):
    row = rows_of((8, 128))
    lane = lax.broadcasted_iota(jnp.int32, (8, 128), 1)

    turn = pl.program_id(0)
    for group in range(STEP_GROUPS):
        u = group_directions(dir_ref, group)
        total = None
        for at in range(LANE_GROUPS // CHUNK):
            left = []
            right = []
            for n in range(CHUNK):
                j = at * CHUNK + n
                turns, weight = group_turns(u, point_ref, j // 2, j % 2)
                powers, step, start = unit_powers(turns)
                high, low = term_rows(powers)
                right.append(jnp.concatenate(high + low, axis=0))
                c, s = weight * start[0], weight * start[1]
                cb, sb = product_conj((c, s), step)
                twice = step[0] + step[0]
                tops = []
                bottoms = []
                for k in range(CENTERS):
                    top, bottom = halves(jnp.concatenate([c, s], axis=0))
                    tops.append(top)
                    bottoms.append(bottom)
                    if k + 1 < CENTERS:
                        c, s, cb, sb = twice * c - cb, twice * s - sb, c, s
                left.append(jnp.concatenate(tops + bottoms, axis=0))
            part = lax.dot_general(
                jnp.concatenate(left, axis=1),
                jnp.concatenate(right, axis=1),
                (((1,), (1,)), ((), ())),
                preferred_element_type=F32,
            )
            total = part if total is None else total + part
        total_ref[turn * STEP_GROUPS + group] = total[0 : 16 * CENTERS] + total[16 * CENTERS :]

    @pl.when(turn == STEPS - 1)
    def _():
        own = (lane & 7) == row
        front = lane < 8 * SIDE
        squares = [jnp.zeros((8, 128), F32)] * 2
        for g in range(GROUPS):
            real = jnp.zeros((8, 128), F32)
            imag = real
            for k in range(CENTERS):
                c = jnp.sum(jnp.where(own, total_ref[g, 16 * k : 16 * k + 8], 0.0), axis=0, keepdims=True)
                s = jnp.sum(jnp.where(own, total_ref[g, 16 * k + 8 : 16 * k + 16], 0.0), axis=0, keepdims=True)
                real = jnp.where(row == k, c, real)
                imag = jnp.where(row == k, s, imag)
            real = (real + pltpu.roll(real, 64, axis=1)) * NORM
            imag = (imag + pltpu.roll(imag, 64, axis=1)) * NORM
            real_sin = pltpu.roll(real, 96, axis=1)
            imag_sin = pltpu.roll(imag, 96, axis=1)
            planes = [real - imag_sin, real + imag_sin, imag + real_sin, imag - real_sin]
            inside = front & ((lane & 7) + g * 8 < DIR_PART)
            planes = [jnp.where(inside, p, 0.0) for p in planes]
            for i in range(4):
                amp_ref[g, i] = planes[i]
            for i in range(2):
                squares[i] = squares[i] + planes[i] * planes[i] + planes[i + 2] * planes[i + 2]
        spread = jnp.zeros((1, 128), F32)
        for i in range(2):
            square = squares[i]
            for shift in (1, 2, 4):
                square = square + pltpu.roll(square, 128 - shift, axis=1)
            for k in range(CENTERS):
                for o in range(SIDE):
                    spread = jnp.where(lane[0:1] == shell_of(i, k, o), square[k : k + 1, 8 * o : 8 * o + 1], spread)
        inten_ref[...] = jnp.broadcast_to(spread, inten_ref.shape)


def point_spec():
    return pl.BlockSpec((PARTS, 4, SOL), lambda g, p: (0, 0, 0))


def direction_spec():
    return pl.BlockSpec((1, 1, 8, 128), lambda g, p: (p[0], g, 0, 0))


def amplitudes(position, points, directions):
    return pl.pallas_call(
        amplitude_kernel,
        grid_spec=pltpu.PrefetchScalarGridSpec(
            num_scalar_prefetch=1,
            grid=(STEPS,),
            in_specs=[point_spec(), direction_spec()],
            out_specs=[
                pl.BlockSpec((GROUPS, 4, 8, 128), lambda g, p: (0, 0, 0, 0)),
                pl.BlockSpec((PARTS * REPLICAS, 128), lambda g, p: (0, 0)),
            ],
            scratch_shapes=[pltpu.VMEM((GROUPS, 16 * CENTERS, 128), F32)],
        ),
        out_shape=[
            jax.ShapeDtypeStruct((GROUPS, 4, 8, 128), F32),
            jax.ShapeDtypeStruct((PARTS * REPLICAS, 128), F32),
        ],
        compiler_params=PARAMS,
        cost_estimate=pl.CostEstimate(flops=10_000_000_000, bytes_accessed=1_000_000, transcendentals=0),
        name="amplitudes",
    )(position, points, directions)


def kick_kernel(position_ref, point_ref, dir_ref, amp_ref, inten_ref, precision_ref, target_ref, out_ref, coef_ref, acc_ref):
    row = rows_of((8, 128))
    lane = lax.broadcasted_iota(jnp.int32, (8, 128), 1)

    @pl.when(pl.program_id(0) == 0)
    def _():
        intensity = jnp.sum(inten_ref[...], axis=0, keepdims=True) * (1.0 / (M * REPLICAS))
        q = 1.0 + lax.broadcasted_iota(jnp.int32, (1, NQ), 1).astype(F32) * (3.0 / NQ)
        factor = precision_ref[...] * (intensity[:, 0:NQ] - target_ref[...]) * (2.0 / M) * q
        scales = []
        for i in range(2):
            scale = jnp.zeros((8, 128), F32)
            for k in range(CENTERS):
                for o in range(SIDE):
                    source = shell_of(i, k, o)
                    here = (row == k) & (lax.shift_right_logical(lane, 3) == o)
                    scale = jnp.where(here, jnp.broadcast_to(factor[:, source : source + 1], (8, 128)), scale)
            scales.append(scale)
        front = lane < 8 * SIDE
        own = (lane & 7) == row
        for g in range(GROUPS):
            b_up = amp_ref[g, 0] * scales[0]
            b_down = amp_ref[g, 1] * scales[1]
            a_up = amp_ref[g, 2] * scales[0]
            a_down = amp_ref[g, 3] * scales[1]
            real = jnp.where(front, a_up + a_down, pltpu.roll(b_down - b_up, 32, axis=1))
            imag = jnp.where(front, b_up + b_down, pltpu.roll(a_up - a_down, 32, axis=1))
            tops = []
            bottoms = []
            for v in (real, imag):
                high = v.astype(BF16).astype(F32)
                tops.append(high + pltpu.roll(high, 64, axis=1))
                bottoms.append(v - high)
            for k in range(CENTERS):
                at = slice(16 * k, 16 * k + 16)
                first = jnp.concatenate([jnp.where(own, v[k : k + 1], 0.0) for v in tops], axis=0).astype(BF16)
                last = jnp.concatenate([jnp.where(own, v[k : k + 1], 0.0) for v in bottoms], axis=0).astype(BF16)
                coef_ref[g, at, 0:128] = first
                coef_ref[g, at, 128:256] = last

    kicked = [[None] * 3 for _ in range(LANE_GROUPS)]
    turn = pl.program_id(0)
    for group in range(STEP_GROUPS):
        u = group_directions(dir_ref, group)

        for at in range(LANE_GROUPS // CHUNK):
            state = []
            columns = []
            for n in range(CHUNK):
                j = at * CHUNK + n
                turns, _ = group_turns(u, point_ref, j // 2, j % 2)
                powers, step, start = unit_powers(turns)
                high, low = term_rows(powers)
                columns.append(jnp.concatenate(high + low + high, axis=0))
                state.append([step, start, step[0] + step[0]])
            terms = jnp.dot(coef_ref[turn * STEP_GROUPS + group, :, 0:192], jnp.concatenate(columns, axis=1), preferred_element_type=F32)
            for n in range(CHUNK):
                step, start, twice = state[n]
                lanes = slice(n * 128, n * 128 + 128)
                r1 = i1 = r2 = i2 = None
                for k in range(CENTERS - 1, -1, -1):
                    real = terms[16 * k : 16 * k + 8, lanes]
                    imag = terms[16 * k + 8 : 16 * k + 16, lanes]
                    if r1 is not None:
                        real = real + twice * r1
                        imag = imag + twice * i1
                    if r2 is not None:
                        real = real - r2
                        imag = imag - i2
                    r1, i1, r2, i2 = real, imag, r1, i1
                real = r1 - r2 * step[0] - i2 * step[1]
                imag = i1 - i2 * step[0] + r2 * step[1]
                slope = real * start[0] - imag * start[1]
                for c in range(3):
                    value = u[c] * slope
                    old = kicked[at * CHUNK + n][c]
                    kicked[at * CHUNK + n][c] = value if old is None else old + value

    @pl.when(turn == 0)
    def _():
        for j in range(LANE_GROUPS):
            for c in range(3):
                acc_ref[3 * j + c] = kicked[j][c]

    @pl.when(turn == STEPS - 1)
    def _():
        for j in range(LANE_GROUPS):
            lanes = slice(j % 2 * 128, j % 2 * 128 + 128)
            for c in range(3):
                total = acc_ref[3 * j + c] + kicked[j][c]
                out_ref[j // 2, c : c + 1, lanes] = jnp.sum(total, axis=0, keepdims=True) * (1.0 / TURN)


def kicks(position, points, directions, amplitude, intensity, shells):
    return pl.pallas_call(
        kick_kernel,
        grid_spec=pltpu.PrefetchScalarGridSpec(
            num_scalar_prefetch=1,
            grid=(STEPS,),
            in_specs=[
                point_spec(),
                direction_spec(),
                pl.BlockSpec((GROUPS, 4, 8, 128), lambda g, p: (0, 0, 0, 0)),
                pl.BlockSpec((PARTS * REPLICAS, 128), lambda g, p: (0, 0)),
                pl.BlockSpec((1, NQ), lambda g, p: (0, 0)),
                pl.BlockSpec((1, NQ), lambda g, p: (0, 0)),
            ],
            out_specs=pl.BlockSpec((PARTS, 3, SOL), lambda g, p: (0, 0, 0)),
            scratch_shapes=[
                pltpu.VMEM((GROUPS, 16 * CENTERS, 256), BF16),
                pltpu.VMEM((LANE_GROUPS * 3, 8, 128), F32),
            ],
        ),
        out_shape=jax.ShapeDtypeStruct((PARTS, 3, SOL), F32),
        compiler_params=PARAMS,
        cost_estimate=pl.CostEstimate(flops=10_000_000_000, bytes_accessed=1_000_000, transcendentals=0),
        name="kicks",
    )(position, points, directions, amplitude, intensity, *shells)


def exchange(head, tail):
    right = [(i, (i + 1) % PARTS) for i in range(PARTS)]
    left = [((i + 1) % PARTS, i) for i in range(PARTS)]
    return lax.ppermute(tail, "sp", right), lax.ppermute(head, "sp", left)


def to_all(value, axes):
    return lax.all_to_all(value, axes, 0, 0, tiled=True)


def shards(
    positions,
    velocities,
    strength,
    inv_mass,
    tile_lists,
    solute_index,
    scatter_weight,
    intensity_exp,
    precision,
):
    position = lax.axis_index("sp").astype(jnp.int32).reshape(1)
    directions = jnp.asarray(direction_table())
    usual = 3 * (jnp.arange(NB, dtype=jnp.int32) + HB)
    tiles = (jnp.sum(tile_lists[0], axis=-1) - usual).reshape(-1)
    shells = (precision.reshape(1, NQ), intensity_exp.reshape(1, NQ))
    state, head, tail, first = pack(
        positions[0], strength, velocities[0], inv_mass, solute_index, scatter_weight
    )
    halo = exchange(head, tail)
    first, halo = lax.optimization_barrier((first, halo))
    first = to_all(first, "sp")
    state, head, tail = pair_step(0, tiles, position, state, halo)
    halo = exchange(head, tail)
    amp, inten = amplitudes(position, first, directions)
    inten = to_all(inten, ("rep", "sp"))
    state, head, tail, second = pair_step(
        1, tiles, position, state, halo, solute_index, scatter_weight, gathers=True
    )
    halo = exchange(head, tail)
    second = to_all(second, "sp")
    kick = to_all(kicks(position, first, directions, amp, inten, shells), "sp")
    amp, inten = amplitudes(position, second, directions)
    inten = to_all(inten, ("rep", "sp"))
    state, head, tail = pair_step(2, tiles, position, state, halo, solute_index, scatter_weight, kick)
    halo = exchange(head, tail)
    kick = to_all(kicks(position, second, directions, amp, inten, shells), "sp")
    place, speed = pair_step(3, tiles, position, state, halo, last=True)
    speed = finish(speed, inv_mass, solute_index, scatter_weight, kick)
    return (place[None], speed[None])


def solution(mesh):
    in_specs = (
        P("rep", None, "sp"),
        P("rep", None, "sp"),
        P("rep", "sp"),
        P("rep", "sp"),
        P("rep", None, "sp", None),
        P("rep", "sp"),
        P("rep", "sp"),
        P(),
        P(),
    )
    out_specs = (P("rep", None, "sp"), P("rep", None, "sp"))
    return jax.shard_map(shards, mesh=mesh, in_specs=in_specs, out_specs=out_specs, check_vma=False)
```

```python
import functools
import math

import jax
import jax.numpy as jnp
import numpy as np
from jax import lax
from jax.experimental import pallas as pl
from jax.experimental.pallas import tpu as pltpu
from jax.sharding import PartitionSpec as P

M = 784
NQ = 48
OUTER = 2
INNER = 2
TIME_STEP = 0.05
PAIR_STRENGTH = 0.2
HALF_INVERSE = 0.03125

BLOCK = 128
NB = 64
HB = 32
EXT = NB + 2 * HB
NEIGHBOURS = 4
ATOMS = NB * BLOCK
HALO = HB * BLOCK
SOL = 256
PARTS = 8
REPLICAS = 16
DIR_PART = M // PARTS
GROUPS = -(-DIR_PART // 8)
STEPS = 2
FULL = GROUPS // STEPS
SLOTS = FULL + 1
SIDE = 4
CENTERS = NQ // (2 * SIDE)
LANE_GROUPS = PARTS * SOL // 128
CHUNK = 4
FILL_UNROLL = 32
BLOCK_UNROLL = 16

ALPHA = math.sqrt(HALF_INVERSE * math.log2(math.e))
COUPLING = PAIR_STRENGTH / math.sqrt(NEIGHBOURS * BLOCK)
NORM = 1.0 / math.sqrt(PARTS * SOL)
TURN = 1.0 / (64.0 * math.pi)

F32 = jnp.float32
BF16 = jnp.bfloat16


def direction_table():
    order = np.arange(M)
    height = 1.0 - (2.0 * order + 1.0) / M
    radius = np.sqrt(1.0 - height * height)
    azimuth = (order * 610 % 987) * (2.0 * math.pi / 987.0)
    rows = np.stack([radius * np.cos(azimuth), radius * np.sin(azimuth), height], axis=-1) * TURN
    padded = np.zeros((PARTS, GROUPS * 8, 3), np.float32)
    padded[:, :DIR_PART] = rows.reshape(PARTS, DIR_PART, 3)
    padded = padded.reshape(PARTS, GROUPS, 8, 3)
    table = np.zeros((PARTS, STEPS, 8, 128), np.float32)
    for turn in range(STEPS):
        for slot in range(SLOTS):
            group = turn * FULL + slot if slot < FULL else GROUPS - 1
            for c in range(3):
                table[:, turn, :, 16 * c + slot] = padded[:, group, :, c]
    return table


def split3(value):
    high = value.astype(BF16).astype(F32)
    rest = value - high
    mid = rest.astype(BF16).astype(F32)
    return high, mid, rest - mid


def halves(value):
    high = value.astype(BF16)
    return high, (value - high.astype(F32)).astype(BF16)


def rows_of(shape):
    return lax.broadcasted_iota(jnp.int32, shape, 0)


def scaled_parts(cell, factor):
    row = rows_of((8, BLOCK))
    scaled = jnp.concatenate([cell, cell], axis=0) * ALPHA
    norm_row = (row & 3) == 3
    norm = -jnp.sum(jnp.where(row < 3, scaled * scaled, 0.0), axis=0, keepdims=True)
    return split3(jnp.where(norm_row, norm, scaled * factor))


def neighbour_features(cell):
    row = rows_of((8, BLOCK))
    both = jnp.concatenate([cell, cell], axis=0)
    charge = jnp.broadcast_to(cell[3:4], (8, BLOCK))
    moments = jnp.where((row & 3) == 3, charge, both * charge)
    th, tm, tl = split3(moments)
    weights = jnp.concatenate([jnp.where(row < 4, th, tm), jnp.where(row < 4, tl, 0.0)], axis=0)
    h, m, l = scaled_parts(cell, 1.0)
    near = [
        jnp.where((row & 3) == 3, 1.0, jnp.where(row < 4, h, m)),
        jnp.where(row < 3, l, jnp.where(row == 3, 1.0, h)),
        jnp.where(row < 4, m, jnp.where(row < 7, h, l)),
        jnp.zeros((8, BLOCK), F32),
    ]
    return jnp.concatenate(near, axis=0).astype(BF16), weights.astype(BF16)


def own_features(cell):
    row = rows_of((8, BLOCK))
    h, m, l = scaled_parts(cell, 2.0)
    own = [
        jnp.where(row == 7, m, h),
        jnp.where(row < 3, h, jnp.where(row == 3, l, jnp.where(row < 7, m, 1.0))),
        jnp.where((row & 3) == 3, 1.0, jnp.where(row < 4, m, l)),
        jnp.zeros((8, BLOCK), F32),
    ]
    return jnp.concatenate(own, axis=0).astype(BF16)


def selectors(index):
    block = lax.shift_right_logical(index, 7)
    lane = index & 127
    by_block = rows_of((NB, SOL)) == block
    by_lane = rows_of((BLOCK, SOL)) == lane
    return by_block, by_lane


def scatter_kicks(index_ref, weight_ref, kick_ref, push_ref):
    by_block, by_lane = selectors(index_ref[...])
    total = kick_ref[0]
    for part in range(1, PARTS):
        total = total + kick_ref[part]
    total = total * (weight_ref[...] * (-INNER * TIME_STEP))
    lanes = jnp.where(by_lane, 1.0, 0.0).astype(BF16)
    lanes = jnp.concatenate([lanes, lanes, lanes], axis=1)
    for c in range(3):
        parts = split3(total[c : c + 1])
        rows = jnp.concatenate([jnp.where(by_block, p, 0.0).astype(BF16) for p in parts], axis=1)
        push_ref[c] = lax.dot_general(rows, lanes, (((1,), (1,)), ((), ())), preferred_element_type=F32)


def gather_points(index_ref, weight_ref, place_ref, point_ref):
    by_block, by_lane = selectors(index_ref[...])
    lanes = jnp.where(by_lane, 1.0, 0.0).astype(BF16)
    found = []
    for c in range(3):
        total = None
        for p in split3(place_ref[c]):
            part = jnp.dot(p.astype(BF16), lanes, preferred_element_type=F32)
            total = part if total is None else total + part
        found.append(jnp.sum(jnp.where(by_block, total, 0.0), axis=0, keepdims=True))
    found.append(weight_ref[...])
    points = jnp.concatenate(found, axis=0)
    for part in range(PARTS):
        point_ref[part] = points


def block_at(b):
    return pl.ds(pl.multiple_of(b * BLOCK, BLOCK), BLOCK)


def pushed(push_ref, b):
    return jnp.concatenate([push_ref[c, pl.ds(b, 1), :] for c in range(3)], axis=0)


def pack_kernel(pos_ref, charge_ref, vel_ref, inverse_ref, index_ref, weight_ref, *refs):
    out_ref, head_ref, tail_ref, point_ref, place_ref = refs

    def one_block(b, carry):
        at = block_at(b)
        place = pos_ref[:, at]
        out_ref[:, at] = jnp.concatenate([place, charge_ref[:, at], vel_ref[:, at], inverse_ref[:, at]], axis=0)
        for c in range(3):
            place_ref[c, pl.ds(b, 1), :] = place[c : c + 1]
        return carry

    lax.fori_loop(0, NB, one_block, 0, unroll=FILL_UNROLL)
    head_ref[...] = out_ref[0:4, 0:HALO]
    tail_ref[...] = out_ref[0:4, HALO:ATOMS]
    gather_points(index_ref, weight_ref, place_ref, point_ref)


def finish_kernel(vel_ref, inverse_ref, index_ref, weight_ref, kick_ref, out_ref, push_ref):
    scatter_kicks(index_ref, weight_ref, kick_ref, push_ref)

    def one_block(b, carry):
        at = block_at(b)
        out_ref[:, at] = vel_ref[:, at] + inverse_ref[:, at] * pushed(push_ref, b)
        return carry

    lax.fori_loop(0, NB, one_block, 0, unroll=FILL_UNROLL)


def pair_kernel(step, kicked, gathers, last, *refs):
    refs = list(refs)
    fourth_ref, position_ref, state_ref, left_ref, right_ref = refs[:5]
    refs = refs[5:]
    if kicked or gathers:
        index_ref, weight_ref = refs[:2]
        refs = refs[2:]
    if kicked:
        kick_ref = refs.pop(0)
    if last:
        pos_ref, vel_ref = refs[:2]
        refs = refs[2:]
    else:
        out_ref, head_ref, tail_ref = refs[:3]
        refs = refs[3:]
    if gathers:
        point_ref = refs.pop(0)
    near_ref, moment_ref = refs[:2]
    refs = refs[2:]
    if gathers:
        place_ref = refs.pop(0)
    if kicked:
        push_ref = refs.pop(0)

    left_ok = jnp.where(position_ref[0] > 0, 1.0, 0.0)
    right_ok = jnp.where(position_ref[0] < PARTS - 1, 1.0, 0.0)
    row4 = rows_of((4, BLOCK))

    def fill(slot, cell):
        near, moments = neighbour_features(cell)
        near_ref[slot] = near.T
        moment_ref[slot] = moments

    def fill_halo(b, carry):
        at = block_at(b)
        fill(b, left_ref[:, at] * jnp.where(row4 == 3, left_ok, 1.0))
        fill(b + HB + NB, right_ref[:, at] * jnp.where(row4 == 3, right_ok, 1.0))
        return carry

    lax.fori_loop(0, HB, fill_halo, 0, unroll=FILL_UNROLL)

    def fill_own(b, carry):
        cell = state_ref[0:4, block_at(b)]
        fill(b + HB, cell)
        return carry

    lax.fori_loop(0, NB, fill_own, 0, unroll=FILL_UNROLL)

    if kicked:
        scatter_kicks(index_ref, weight_ref, kick_ref, push_ref)

    def update(b, cell, sums):
        sums = sums[0:4] + sums[4:8] + sums[8:12]
        at = block_at(b)
        place, charge, speed, inverse = cell[0:3], cell[3:4], cell[4:7], cell[7:8]
        force = (COUPLING * charge) * (place * sums[3:4] - sums[0:3])
        if kicked:
            speed = speed + inverse * pushed(push_ref, b)
        speed = speed + (TIME_STEP * inverse) * force
        place = place + TIME_STEP * speed
        if gathers:
            for c in range(3):
                place_ref[c, pl.ds(b, 1), :] = place[c : c + 1]
        if last:
            pos_ref[:, at] = place
            vel_ref[:, at] = speed
        else:
            out_ref[:, at] = jnp.concatenate([place, charge, speed, inverse], axis=0)

    def weighted(first, second, own):
        near = jnp.concatenate([near_ref[first], near_ref[second]], axis=0)
        moments = jnp.concatenate([moment_ref[first], moment_ref[second]], axis=1)
        high, low = halves(jnp.exp2(jnp.dot(near, own, preferred_element_type=F32)))
        sums = jnp.dot(moments, high, preferred_element_type=F32)
        return sums + jnp.dot(moments, low, preferred_element_type=F32)

    def one_pair(b, carry):
        c = b + HB
        cells = [state_ref[:, block_at(b)], state_ref[:, block_at(c)]]
        own = [own_features(v[0:4]) for v in cells]
        shared = weighted(b + HB, b + 2 * HB, jnp.concatenate(own, axis=1))
        left = weighted(b, fourth_ref[step * NB + b], own[0])
        right = weighted(b + 3 * HB, fourth_ref[step * NB + c], own[1])
        update(b, cells[0], shared[:, 0:BLOCK] + left)
        update(c, cells[1], shared[:, BLOCK:] + right)
        return carry

    lax.fori_loop(0, HB, one_pair, 0, unroll=BLOCK_UNROLL)

    if not last:
        head_ref[...] = out_ref[0:4, 0:HALO]
        tail_ref[...] = out_ref[0:4, HALO:ATOMS]
    if gathers:
        gather_points(index_ref, weight_ref, place_ref, point_ref)


VMEM = pl.BlockSpec(memory_space=pltpu.VMEM)
SMEM = pl.BlockSpec(memory_space=pltpu.SMEM)
PARAMS = pltpu.CompilerParams(vmem_limit_bytes=32 << 20)


def pack(positions, strength, velocities, inv_mass, index, weights):
    return pl.pallas_call(
        pack_kernel,
        out_shape=[
            jax.ShapeDtypeStruct((8, ATOMS), F32),
            jax.ShapeDtypeStruct((4, HALO), F32),
            jax.ShapeDtypeStruct((4, HALO), F32),
            jax.ShapeDtypeStruct((PARTS, 4, SOL), F32),
        ],
        in_specs=[VMEM] * 6,
        out_specs=[VMEM] * 4,
        scratch_shapes=[pltpu.VMEM((3, NB, BLOCK), F32)],
        compiler_params=PARAMS,
        cost_estimate=pl.CostEstimate(flops=100_000_000, bytes_accessed=600_000, transcendentals=0),
        name="pack",
    )(positions, strength, velocities, inv_mass, index, weights)


def finish(velocities, inv_mass, index, weights, kick):
    return pl.pallas_call(
        finish_kernel,
        out_shape=jax.ShapeDtypeStruct((3, ATOMS), F32),
        in_specs=[VMEM] * 5,
        out_specs=VMEM,
        scratch_shapes=[pltpu.VMEM((3, NB, BLOCK), F32)],
        compiler_params=PARAMS,
        cost_estimate=pl.CostEstimate(flops=100_000_000, bytes_accessed=300_000, transcendentals=0),
        name="finish",
    )(velocities, inv_mass, index, weights, kick)


def pair_step(step, tiles, position, state, halo, index=None, weights=None, kick=None, gathers=False, last=False):
    kicked = kick is not None
    operands = [tiles, position, state, halo[0], halo[1]]
    specs = [SMEM, SMEM, VMEM, VMEM, VMEM]
    if kicked or gathers:
        operands += [index, weights]
        specs += [VMEM, VMEM]
    if kicked:
        operands.append(kick)
        specs.append(VMEM)
    scratch = [
        pltpu.VMEM((EXT, BLOCK, 32), BF16),
        pltpu.VMEM((EXT, 16, BLOCK), BF16),
    ]
    if last:
        shapes = [jax.ShapeDtypeStruct((3, ATOMS), F32)] * 2
    else:
        shapes = [jax.ShapeDtypeStruct((8, ATOMS), F32)] + [jax.ShapeDtypeStruct((4, HALO), F32)] * 2
    if gathers:
        shapes.append(jax.ShapeDtypeStruct((PARTS, 4, SOL), F32))
        scratch.append(pltpu.VMEM((3, NB, BLOCK), F32))
    if kicked:
        scratch.append(pltpu.VMEM((3, NB, BLOCK), F32))
    return pl.pallas_call(
        functools.partial(pair_kernel, step, kicked, gathers, last),
        out_shape=shapes,
        in_specs=specs,
        out_specs=[VMEM] * len(shapes),
        scratch_shapes=scratch,
        compiler_params=PARAMS,
        cost_estimate=pl.CostEstimate(flops=6_000_000_000, bytes_accessed=2_000_000, transcendentals=4_000_000),
        name="pair_step",
    )(*operands)


def double(cos, sin):
    twice = sin + sin
    return 1.0 - twice * sin, twice * cos


def product(a, b):
    return a[0] * b[0] - a[1] * b[1], a[1] * b[0] + a[0] * b[1]


def product_conj(a, b):
    return a[0] * b[0] + a[1] * b[1], a[1] * b[0] - a[0] * b[1]


def unit_powers(turns):
    y = (turns - jnp.round(turns)) * (0.5 * math.pi)
    z = y * y
    sin = ((-1.9515295891e-4 * z + 8.3321608736e-3) * z - 1.6666654611e-1) * (z * y) + y
    cos = ((2.443315711809948e-5 * z - 1.388731625493765e-3) * z + 4.166664568298827e-2) * (z * z) + (1.0 - 0.5 * z)
    one = double(*double(cos, sin))
    two = double(*one)
    three = product(two, one)
    five = product(three, two)
    seven = product(five, two)
    sixteen = double(*double(*double(*two)))
    return [one, three, five, seven], sixteen, product(double(*sixteen), seven)


def term_rows(powers):
    values = [p[0] for p in powers] + [p[1] for p in powers]
    parts = [halves(jnp.concatenate(values[i : i + 2], axis=0)) for i in range(0, 8, 2)]
    return [p[0] for p in parts], [p[1] for p in parts]


def group_directions(dir_ref, group):
    return [jnp.broadcast_to(dir_ref[0, 0, :, 16 * c + group : 16 * c + group + 1], (8, 128)) for c in range(3)]


def group_turns(u, point_ref, part, half):
    lanes = slice(half * 128, half * 128 + 128)

    def coordinate(c):
        return jnp.broadcast_to(point_ref[part, c : c + 1, lanes], (8, 128))

    return u[0] * coordinate(0) + u[1] * coordinate(1) + u[2] * coordinate(2), coordinate(3)


def shell_of(down, k, o):
    return 8 * k + 3 - o if down else 8 * k + 4 + o


def amplitude_kernel(position_ref, point_ref, dir_ref, amp_ref, inten_ref, total_ref):
    row = rows_of((8, 128))
    lane = lax.broadcasted_iota(jnp.int32, (8, 128), 1)

    turn = pl.program_id(0)
    for slot in range(SLOTS):
        u = group_directions(dir_ref, slot)
        total = None
        for at in chunks_of(slot):
            left = []
            right = []
            for n in range(CHUNK):
                turns, weight = group_turns(u, point_ref, part_of(turn, slot, at, n), n % 2)
                powers, step, start = unit_powers(turns)
                high, low = term_rows(powers)
                right.append(jnp.concatenate(high + low, axis=0))
                c, s = weight * start[0], weight * start[1]
                cb, sb = product_conj((c, s), step)
                twice = step[0] + step[0]
                tops = []
                bottoms = []
                for k in range(CENTERS):
                    top, bottom = halves(jnp.concatenate([c, s], axis=0))
                    tops.append(top)
                    bottoms.append(bottom)
                    if k + 1 < CENTERS:
                        c, s, cb, sb = twice * c - cb, twice * s - sb, c, s
                left.append(jnp.concatenate(tops + bottoms, axis=0))
            part = lax.dot_general(
                jnp.concatenate(left, axis=1),
                jnp.concatenate(right, axis=1),
                (((1,), (1,)), ((), ())),
                preferred_element_type=F32,
            )
            total = part if total is None else total + part
        total_ref[turn * SLOTS + slot] = total[0 : 16 * CENTERS] + total[16 * CENTERS :]

    @pl.when(turn == STEPS - 1)
    def _():
        own = (lane & 7) == row
        front = lane < 8 * SIDE
        squares = [jnp.zeros((8, 128), F32)] * 2
        for g in range(GROUPS):
            if g < GROUPS - 1:
                sums = total_ref[g // FULL * SLOTS + g % FULL]
            else:
                sums = total_ref[FULL] + total_ref[SLOTS + FULL]
            real = jnp.zeros((8, 128), F32)
            imag = real
            for k in range(CENTERS):
                c = jnp.sum(jnp.where(own, sums[16 * k : 16 * k + 8], 0.0), axis=0, keepdims=True)
                s = jnp.sum(jnp.where(own, sums[16 * k + 8 : 16 * k + 16], 0.0), axis=0, keepdims=True)
                real = jnp.where(row == k, c, real)
                imag = jnp.where(row == k, s, imag)
            real = (real + pltpu.roll(real, 64, axis=1)) * NORM
            imag = (imag + pltpu.roll(imag, 64, axis=1)) * NORM
            real_sin = pltpu.roll(real, 96, axis=1)
            imag_sin = pltpu.roll(imag, 96, axis=1)
            planes = [real - imag_sin, real + imag_sin, imag + real_sin, imag - real_sin]
            inside = front & ((lane & 7) + g * 8 < DIR_PART)
            planes = [jnp.where(inside, p, 0.0) for p in planes]
            for i in range(4):
                amp_ref[g, i] = planes[i]
            for i in range(2):
                squares[i] = squares[i] + planes[i] * planes[i] + planes[i + 2] * planes[i + 2]
        spread = jnp.zeros((1, 128), F32)
        for i in range(2):
            square = squares[i]
            for shift in (1, 2, 4):
                square = square + pltpu.roll(square, 128 - shift, axis=1)
            for k in range(CENTERS):
                for o in range(SIDE):
                    spread = jnp.where(lane[0:1] == shell_of(i, k, o), square[k : k + 1, 8 * o : 8 * o + 1], spread)
        inten_ref[...] = jnp.broadcast_to(spread, inten_ref.shape)


def chunks_of(slot):
    return range(LANE_GROUPS // CHUNK if slot < FULL else LANE_GROUPS // CHUNK // STEPS)


def part_of(turn, slot, at, n):
    part = (at * CHUNK + n) // 2
    return part if slot < FULL else turn * (PARTS // STEPS) + part


def point_spec():
    return pl.BlockSpec((PARTS, 4, SOL), lambda g, p: (0, 0, 0))


def direction_spec():
    return pl.BlockSpec((1, 1, 8, 128), lambda g, p: (p[0], g, 0, 0))


def amplitudes(position, points, directions):
    return pl.pallas_call(
        amplitude_kernel,
        grid_spec=pltpu.PrefetchScalarGridSpec(
            num_scalar_prefetch=1,
            grid=(STEPS,),
            in_specs=[point_spec(), direction_spec()],
            out_specs=[
                pl.BlockSpec((GROUPS, 4, 8, 128), lambda g, p: (0, 0, 0, 0)),
                pl.BlockSpec((PARTS * REPLICAS, 128), lambda g, p: (0, 0)),
            ],
            scratch_shapes=[pltpu.VMEM((STEPS * SLOTS, 16 * CENTERS, 128), F32)],
        ),
        out_shape=[
            jax.ShapeDtypeStruct((GROUPS, 4, 8, 128), F32),
            jax.ShapeDtypeStruct((PARTS * REPLICAS, 128), F32),
        ],
        compiler_params=PARAMS,
        cost_estimate=pl.CostEstimate(flops=10_000_000_000, bytes_accessed=1_000_000, transcendentals=0),
        name="amplitudes",
    )(position, points, directions)


def kick_kernel(position_ref, point_ref, dir_ref, amp_ref, inten_ref, precision_ref, target_ref, out_ref, coef_ref, acc_ref):
    row = rows_of((8, 128))
    lane = lax.broadcasted_iota(jnp.int32, (8, 128), 1)

    @pl.when(pl.program_id(0) == 0)
    def _():
        intensity = jnp.sum(inten_ref[...], axis=0, keepdims=True) * (1.0 / (M * REPLICAS))
        q = 1.0 + lax.broadcasted_iota(jnp.int32, (1, NQ), 1).astype(F32) * (3.0 / NQ)
        factor = precision_ref[...] * (intensity[:, 0:NQ] - target_ref[...]) * (2.0 / M) * q
        scales = []
        for i in range(2):
            scale = jnp.zeros((8, 128), F32)
            for k in range(CENTERS):
                for o in range(SIDE):
                    source = shell_of(i, k, o)
                    here = (row == k) & (lax.shift_right_logical(lane, 3) == o)
                    scale = jnp.where(here, jnp.broadcast_to(factor[:, source : source + 1], (8, 128)), scale)
            scales.append(scale)
        front = lane < 8 * SIDE
        own = (lane & 7) == row
        for g in range(GROUPS):
            b_up = amp_ref[g, 0] * scales[0]
            b_down = amp_ref[g, 1] * scales[1]
            a_up = amp_ref[g, 2] * scales[0]
            a_down = amp_ref[g, 3] * scales[1]
            real = jnp.where(front, a_up + a_down, pltpu.roll(b_down - b_up, 32, axis=1))
            imag = jnp.where(front, b_up + b_down, pltpu.roll(a_up - a_down, 32, axis=1))
            tops = []
            bottoms = []
            for v in (real, imag):
                high = v.astype(BF16).astype(F32)
                tops.append(high + pltpu.roll(high, 64, axis=1))
                bottoms.append(v - high)
            for k in range(CENTERS):
                at = slice(16 * k, 16 * k + 16)
                first = jnp.concatenate([jnp.where(own, v[k : k + 1], 0.0) for v in tops], axis=0).astype(BF16)
                last = jnp.concatenate([jnp.where(own, v[k : k + 1], 0.0) for v in bottoms], axis=0).astype(BF16)
                coef_ref[g, at, 0:128] = first
                coef_ref[g, at, 128:256] = last

    kicked = [[None] * 3 for _ in range(LANE_GROUPS)]
    halved = [[None] * 3 for _ in range(LANE_GROUPS // STEPS)]
    turn = pl.program_id(0)
    for slot in range(SLOTS):
        u = group_directions(dir_ref, slot)
        held = kicked if slot < FULL else halved
        group = turn * FULL + slot if slot < FULL else GROUPS - 1

        for at in chunks_of(slot):
            state = []
            columns = []
            for n in range(CHUNK):
                turns, _ = group_turns(u, point_ref, part_of(turn, slot, at, n), n % 2)
                powers, step, start = unit_powers(turns)
                high, low = term_rows(powers)
                columns.append(jnp.concatenate(high + low + high, axis=0))
                state.append([step, start, step[0] + step[0]])
            terms = jnp.dot(coef_ref[group, :, 0:192], jnp.concatenate(columns, axis=1), preferred_element_type=F32)
            for n in range(CHUNK):
                step, start, twice = state[n]
                lanes = slice(n * 128, n * 128 + 128)
                r1 = i1 = r2 = i2 = None
                for k in range(CENTERS - 1, -1, -1):
                    real = terms[16 * k : 16 * k + 8, lanes]
                    imag = terms[16 * k + 8 : 16 * k + 16, lanes]
                    if r1 is not None:
                        real = real + twice * r1
                        imag = imag + twice * i1
                    if r2 is not None:
                        real = real - r2
                        imag = imag - i2
                    r1, i1, r2, i2 = real, imag, r1, i1
                real = r1 - r2 * step[0] - i2 * step[1]
                imag = i1 - i2 * step[0] + r2 * step[1]
                slope = real * start[0] - imag * start[1]
                for c in range(3):
                    value = u[c] * slope
                    old = held[at * CHUNK + n][c]
                    held[at * CHUNK + n][c] = value if old is None else old + value

    @pl.when(turn == 0)
    def _():
        for j in range(LANE_GROUPS):
            for c in range(3):
                acc_ref[3 * j + c] = kicked[j][c]

    for j in range(LANE_GROUPS // STEPS):
        for c in range(3):
            acc_ref[3 * (turn * (LANE_GROUPS // STEPS) + j) + c] += halved[j][c]

    @pl.when(turn == STEPS - 1)
    def _():
        for j in range(LANE_GROUPS):
            lanes = slice(j % 2 * 128, j % 2 * 128 + 128)
            for c in range(3):
                total = acc_ref[3 * j + c] + kicked[j][c]
                out_ref[j // 2, c : c + 1, lanes] = jnp.sum(total, axis=0, keepdims=True) * (1.0 / TURN)


def kicks(position, points, directions, amplitude, intensity, shells):
    return pl.pallas_call(
        kick_kernel,
        grid_spec=pltpu.PrefetchScalarGridSpec(
            num_scalar_prefetch=1,
            grid=(STEPS,),
            in_specs=[
                point_spec(),
                direction_spec(),
                pl.BlockSpec((GROUPS, 4, 8, 128), lambda g, p: (0, 0, 0, 0)),
                pl.BlockSpec((PARTS * REPLICAS, 128), lambda g, p: (0, 0)),
                pl.BlockSpec((1, NQ), lambda g, p: (0, 0)),
                pl.BlockSpec((1, NQ), lambda g, p: (0, 0)),
            ],
            out_specs=pl.BlockSpec((PARTS, 3, SOL), lambda g, p: (0, 0, 0)),
            scratch_shapes=[
                pltpu.VMEM((GROUPS, 16 * CENTERS, 256), BF16),
                pltpu.VMEM((LANE_GROUPS * 3, 8, 128), F32),
            ],
        ),
        out_shape=jax.ShapeDtypeStruct((PARTS, 3, SOL), F32),
        compiler_params=PARAMS,
        cost_estimate=pl.CostEstimate(flops=10_000_000_000, bytes_accessed=1_000_000, transcendentals=0),
        name="kicks",
    )(position, points, directions, amplitude, intensity, *shells)


def exchange(head, tail):
    right = [(i, (i + 1) % PARTS) for i in range(PARTS)]
    left = [((i + 1) % PARTS, i) for i in range(PARTS)]
    return lax.ppermute(tail, "sp", right), lax.ppermute(head, "sp", left)


def to_all(value, axes):
    return lax.all_to_all(value, axes, 0, 0, tiled=True)


def shards(
    positions,
    velocities,
    strength,
    inv_mass,
    tile_lists,
    solute_index,
    scatter_weight,
    intensity_exp,
    precision,
):
    position = lax.axis_index("sp").astype(jnp.int32).reshape(1)
    directions = jnp.asarray(direction_table())
    usual = 3 * (jnp.arange(NB, dtype=jnp.int32) + HB)
    tiles = (jnp.sum(tile_lists[0], axis=-1) - usual).reshape(-1)
    shells = (precision.reshape(1, NQ), intensity_exp.reshape(1, NQ))
    state, head, tail, first = pack(
        positions[0], strength, velocities[0], inv_mass, solute_index, scatter_weight
    )
    halo = exchange(head, tail)
    first, halo = lax.optimization_barrier((first, halo))
    first = to_all(first, "sp")
    state, head, tail = pair_step(0, tiles, position, state, halo)
    halo = exchange(head, tail)
    amp, inten = amplitudes(position, first, directions)
    inten = to_all(inten, ("rep", "sp"))
    state, head, tail, second = pair_step(
        1, tiles, position, state, halo, solute_index, scatter_weight, gathers=True
    )
    halo = exchange(head, tail)
    second = to_all(second, "sp")
    kick = to_all(kicks(position, first, directions, amp, inten, shells), "sp")
    amp, inten = amplitudes(position, second, directions)
    inten = to_all(inten, ("rep", "sp"))
    state, head, tail = pair_step(2, tiles, position, state, halo, solute_index, scatter_weight, kick)
    halo = exchange(head, tail)
    kick = to_all(kicks(position, second, directions, amp, inten, shells), "sp")
    place, speed = pair_step(3, tiles, position, state, halo, last=True)
    speed = finish(speed, inv_mass, solute_index, scatter_weight, kick)
    return (place[None], speed[None])


def solution(mesh):
    in_specs = (
        P("rep", None, "sp"),
        P("rep", None, "sp"),
        P("rep", "sp"),
        P("rep", "sp"),
        P("rep", None, "sp", None),
        P("rep", "sp"),
        P("rep", "sp"),
        P(),
        P(),
    )
    out_specs = (P("rep", None, "sp"), P("rep", None, "sp"))
    return jax.shard_map(shards, mesh=mesh, in_specs=in_specs, out_specs=out_specs, check_vma=False)
```

```python
import functools
import math

import jax
import jax.numpy as jnp
import numpy as np
from jax import lax
from jax.experimental import pallas as pl
from jax.experimental.pallas import tpu as pltpu
from jax.sharding import PartitionSpec as P

M = 784
NQ = 48
OUTER = 2
INNER = 2
TIME_STEP = 0.05
PAIR_STRENGTH = 0.2
HALF_INVERSE = 0.03125

BLOCK = 128
NB = 64
HB = 32
EXT = NB + 2 * HB
NEIGHBOURS = 4
ATOMS = NB * BLOCK
HALO = HB * BLOCK
SOL = 256
PARTS = 8
REPLICAS = 16
DIR_PART = M // PARTS
GROUPS = -(-DIR_PART // 8)
STEPS = 2
FULL = GROUPS // STEPS
SLOTS = FULL + 1
SIDE = 4
CENTERS = NQ // (2 * SIDE)
LANE_GROUPS = PARTS * SOL // 128
CHUNK = 4
FILL_UNROLL = 32
BLOCK_UNROLL = 16

ALPHA = math.sqrt(HALF_INVERSE * math.log2(math.e))
COUPLING = PAIR_STRENGTH / math.sqrt(NEIGHBOURS * BLOCK)
NORM = 1.0 / math.sqrt(PARTS * SOL)
TURN = 1.0 / (64.0 * math.pi)

F32 = jnp.float32
BF16 = jnp.bfloat16


def direction_table():
    order = np.arange(M)
    height = 1.0 - (2.0 * order + 1.0) / M
    radius = np.sqrt(1.0 - height * height)
    azimuth = (order * 610 % 987) * (2.0 * math.pi / 987.0)
    rows = np.stack([radius * np.cos(azimuth), radius * np.sin(azimuth), height], axis=-1) * TURN
    padded = np.zeros((PARTS, GROUPS * 8, 3), np.float32)
    padded[:, :DIR_PART] = rows.reshape(PARTS, DIR_PART, 3)
    padded = padded.reshape(PARTS, GROUPS, 8, 3)
    table = np.zeros((PARTS, STEPS, 8, 128), np.float32)
    for turn in range(STEPS):
        for slot in range(SLOTS):
            group = turn * FULL + slot if slot < FULL else GROUPS - 1
            for c in range(3):
                table[:, turn, :, 16 * c + slot] = padded[:, group, :, c]
    return table


def split3(value):
    high = value.astype(BF16).astype(F32)
    rest = value - high
    mid = rest.astype(BF16).astype(F32)
    return high, mid, rest - mid


def halves(value):
    high = value.astype(BF16)
    return high, (value - high.astype(F32)).astype(BF16)


def rows_of(shape):
    return lax.broadcasted_iota(jnp.int32, shape, 0)


def scaled_parts(cell, factor):
    row = rows_of((8, BLOCK))
    scaled = jnp.concatenate([cell, cell], axis=0) * ALPHA
    norm_row = (row & 3) == 3
    norm = -jnp.sum(jnp.where(row < 3, scaled * scaled, 0.0), axis=0, keepdims=True)
    return split3(jnp.where(norm_row, norm, scaled * factor))


def neighbour_features(cell):
    row = rows_of((8, BLOCK))
    both = jnp.concatenate([cell, cell], axis=0)
    charge = jnp.broadcast_to(cell[3:4], (8, BLOCK))
    moments = jnp.where((row & 3) == 3, charge, both * charge)
    th, tm, tl = split3(moments)
    weights = jnp.concatenate([jnp.where(row < 4, th, tm), jnp.where(row < 4, tl, 0.0)], axis=0)
    h, m, l = scaled_parts(cell, 1.0)
    near = [
        jnp.where((row & 3) == 3, 1.0, jnp.where(row < 4, h, m)),
        jnp.where(row < 3, l, jnp.where(row == 3, 1.0, h)),
        jnp.where(row < 4, m, jnp.where(row < 7, h, l)),
        jnp.zeros((8, BLOCK), F32),
    ]
    return jnp.concatenate(near, axis=0).astype(BF16), weights.astype(BF16)


def own_features(cell):
    row = rows_of((8, BLOCK))
    h, m, l = scaled_parts(cell, 2.0)
    own = [
        jnp.where(row == 7, m, h),
        jnp.where(row < 3, h, jnp.where(row == 3, l, jnp.where(row < 7, m, 1.0))),
        jnp.where((row & 3) == 3, 1.0, jnp.where(row < 4, m, l)),
        jnp.zeros((8, BLOCK), F32),
    ]
    return jnp.concatenate(own, axis=0).astype(BF16)


def selectors(index):
    block = lax.shift_right_logical(index, 7)
    lane = index & 127
    by_block = rows_of((NB, SOL)) == block
    by_lane = rows_of((BLOCK, SOL)) == lane
    return by_block, by_lane


def scatter_kicks(index_ref, weight_ref, kick_ref, push_ref):
    by_block, by_lane = selectors(index_ref[...])
    total = kick_ref[0]
    for part in range(1, PARTS):
        total = total + kick_ref[part]
    total = total * (weight_ref[...] * (-INNER * TIME_STEP))
    lanes = jnp.where(by_lane, 1.0, 0.0).astype(BF16)
    lanes = jnp.concatenate([lanes, lanes, lanes], axis=1)
    for c in range(3):
        parts = split3(total[c : c + 1])
        rows = jnp.concatenate([jnp.where(by_block, p, 0.0).astype(BF16) for p in parts], axis=1)
        push_ref[c] = lax.dot_general(rows, lanes, (((1,), (1,)), ((), ())), preferred_element_type=F32)


def gather_points(index_ref, weight_ref, place_ref, point_ref):
    by_block, by_lane = selectors(index_ref[...])
    lanes = jnp.where(by_lane, 1.0, 0.0).astype(BF16)
    found = []
    for c in range(3):
        total = None
        for p in split3(place_ref[c]):
            part = jnp.dot(p.astype(BF16), lanes, preferred_element_type=F32)
            total = part if total is None else total + part
        found.append(jnp.sum(jnp.where(by_block, total, 0.0), axis=0, keepdims=True))
    found.append(weight_ref[...])
    points = jnp.concatenate(found, axis=0)
    for part in range(PARTS):
        point_ref[part, :, 0:SOL] = points


def block_at(b):
    return pl.ds(pl.multiple_of(b * BLOCK, BLOCK), BLOCK)


def pushed(push_ref, b):
    return jnp.concatenate([push_ref[c, pl.ds(b, 1), :] for c in range(3)], axis=0)


def pack_kernel(pos_ref, charge_ref, vel_ref, inverse_ref, index_ref, weight_ref, *refs):
    out_ref, head_ref, tail_ref, point_ref, place_ref = refs

    def one_block(b, carry):
        at = block_at(b)
        place = pos_ref[:, at]
        out_ref[:, at] = jnp.concatenate([place, charge_ref[:, at], vel_ref[:, at], inverse_ref[:, at]], axis=0)
        for c in range(3):
            place_ref[c, pl.ds(b, 1), :] = place[c : c + 1]
        return carry

    lax.fori_loop(0, NB, one_block, 0, unroll=FILL_UNROLL)
    head_ref[...] = out_ref[0:4, 0:HALO]
    tail_ref[...] = out_ref[0:4, HALO:ATOMS]
    gather_points(index_ref, weight_ref, place_ref, point_ref)


def finish_kernel(vel_ref, inverse_ref, index_ref, weight_ref, kick_ref, out_ref, push_ref):
    scatter_kicks(index_ref, weight_ref, kick_ref, push_ref)

    def one_block(b, carry):
        at = block_at(b)
        out_ref[:, at] = vel_ref[:, at] + inverse_ref[:, at] * pushed(push_ref, b)
        return carry

    lax.fori_loop(0, NB, one_block, 0, unroll=FILL_UNROLL)


def pair_kernel(step, kicked, gathers, last, merged, *refs):
    refs = list(refs)
    fourth_ref, position_ref, state_ref, left_ref, right_ref = refs[:5]
    refs = refs[5:]
    if merged:
        both_ref = left_ref
        left_ref = both_ref.at[lax.rem(position_ref[0] + PARTS - 1, PARTS), :, SOL : SOL + HALO]
        right_ref = both_ref.at[lax.rem(position_ref[0] + 1, PARTS), :, SOL : SOL + HALO]
    if kicked or gathers:
        index_ref, weight_ref = refs[:2]
        refs = refs[2:]
    if kicked:
        kick_ref = refs.pop(0)
    if last:
        pos_ref, vel_ref = refs[:2]
        refs = refs[2:]
    elif gathers:
        out_ref, point_ref = refs[:2]
        refs = refs[2:]
    else:
        out_ref, head_ref, tail_ref = refs[:3]
        refs = refs[3:]
    near_ref, moment_ref = refs[:2]
    refs = refs[2:]
    if gathers:
        place_ref = refs.pop(0)
    if kicked:
        push_ref = refs.pop(0)

    left_ok = jnp.where(position_ref[0] > 0, 1.0, 0.0)
    right_ok = jnp.where(position_ref[0] < PARTS - 1, 1.0, 0.0)
    row4 = rows_of((4, BLOCK))

    def fill(slot, cell):
        near, moments = neighbour_features(cell)
        near_ref[slot] = near.T
        moment_ref[slot] = moments

    def fill_halo(b, carry):
        at = block_at(b)
        fill(b, left_ref[:, at] * jnp.where(row4 == 3, left_ok, 1.0))
        fill(b + HB + NB, right_ref[:, at] * jnp.where(row4 == 3, right_ok, 1.0))
        return carry

    lax.fori_loop(0, HB, fill_halo, 0, unroll=FILL_UNROLL)

    def fill_own(b, carry):
        cell = state_ref[0:4, block_at(b)]
        fill(b + HB, cell)
        return carry

    lax.fori_loop(0, NB, fill_own, 0, unroll=FILL_UNROLL)

    if kicked:
        scatter_kicks(index_ref, weight_ref, kick_ref, push_ref)

    def update(b, cell, sums):
        sums = sums[0:4] + sums[4:8] + sums[8:12]
        at = block_at(b)
        place, charge, speed, inverse = cell[0:3], cell[3:4], cell[4:7], cell[7:8]
        force = (COUPLING * charge) * (place * sums[3:4] - sums[0:3])
        if kicked:
            speed = speed + inverse * pushed(push_ref, b)
        speed = speed + (TIME_STEP * inverse) * force
        place = place + TIME_STEP * speed
        if gathers:
            for c in range(3):
                place_ref[c, pl.ds(b, 1), :] = place[c : c + 1]
        if last:
            pos_ref[:, at] = place
            vel_ref[:, at] = speed
        else:
            out_ref[:, at] = jnp.concatenate([place, charge, speed, inverse], axis=0)

    def weighted(first, second, own):
        near = jnp.concatenate([near_ref[first], near_ref[second]], axis=0)
        moments = jnp.concatenate([moment_ref[first], moment_ref[second]], axis=1)
        high, low = halves(jnp.exp2(jnp.dot(near, own, preferred_element_type=F32)))
        sums = jnp.dot(moments, high, preferred_element_type=F32)
        return sums + jnp.dot(moments, low, preferred_element_type=F32)

    def one_pair(b, carry):
        c = b + HB
        cells = [state_ref[:, block_at(b)], state_ref[:, block_at(c)]]
        own = [own_features(v[0:4]) for v in cells]
        shared = weighted(b + HB, b + 2 * HB, jnp.concatenate(own, axis=1))
        left = weighted(b, fourth_ref[step * NB + b], own[0])
        right = weighted(b + 3 * HB, fourth_ref[step * NB + c], own[1])
        update(b, cells[0], shared[:, 0:BLOCK] + left)
        update(c, cells[1], shared[:, BLOCK:] + right)
        return carry

    lax.fori_loop(0, HB, one_pair, 0, unroll=BLOCK_UNROLL)

    if gathers:
        position = position_ref[0]
        up = lax.rem(position + 1, PARTS)
        down = lax.rem(position + PARTS - 1, PARTS)
        point_ref[down, :, SOL : SOL + HALO] = out_ref[0:4, 0:HALO]
        point_ref[up, :, SOL : SOL + HALO] = out_ref[0:4, HALO:ATOMS]
    elif not last:
        head_ref[...] = out_ref[0:4, 0:HALO]
        tail_ref[...] = out_ref[0:4, HALO:ATOMS]
    if gathers:
        gather_points(index_ref, weight_ref, place_ref, point_ref)


VMEM = pl.BlockSpec(memory_space=pltpu.VMEM)
SMEM = pl.BlockSpec(memory_space=pltpu.SMEM)
PARAMS = pltpu.CompilerParams(vmem_limit_bytes=32 << 20)


def pack(positions, strength, velocities, inv_mass, index, weights):
    return pl.pallas_call(
        pack_kernel,
        out_shape=[
            jax.ShapeDtypeStruct((8, ATOMS), F32),
            jax.ShapeDtypeStruct((4, HALO), F32),
            jax.ShapeDtypeStruct((4, HALO), F32),
            jax.ShapeDtypeStruct((PARTS, 4, SOL), F32),
        ],
        in_specs=[VMEM] * 6,
        out_specs=[VMEM] * 4,
        scratch_shapes=[pltpu.VMEM((3, NB, BLOCK), F32)],
        compiler_params=PARAMS,
        cost_estimate=pl.CostEstimate(flops=100_000_000, bytes_accessed=600_000, transcendentals=0),
        name="pack",
    )(positions, strength, velocities, inv_mass, index, weights)


def finish(velocities, inv_mass, index, weights, kick):
    return pl.pallas_call(
        finish_kernel,
        out_shape=jax.ShapeDtypeStruct((3, ATOMS), F32),
        in_specs=[VMEM] * 5,
        out_specs=VMEM,
        scratch_shapes=[pltpu.VMEM((3, NB, BLOCK), F32)],
        compiler_params=PARAMS,
        cost_estimate=pl.CostEstimate(flops=100_000_000, bytes_accessed=300_000, transcendentals=0),
        name="finish",
    )(velocities, inv_mass, index, weights, kick)


def pair_step(step, tiles, position, state, halo, index=None, weights=None, kick=None, gathers=False, last=False):
    kicked = kick is not None
    operands = [tiles, position, state, halo[0], halo[1]]
    specs = [SMEM, SMEM, VMEM, VMEM, VMEM]
    if kicked or gathers:
        operands += [index, weights]
        specs += [VMEM, VMEM]
    if kicked:
        operands.append(kick)
        specs.append(VMEM)
    scratch = [
        pltpu.VMEM((EXT, BLOCK, 32), BF16),
        pltpu.VMEM((EXT, 16, BLOCK), BF16),
    ]
    if last:
        shapes = [jax.ShapeDtypeStruct((3, ATOMS), F32)] * 2
    elif gathers:
        shapes = [jax.ShapeDtypeStruct((8, ATOMS), F32), jax.ShapeDtypeStruct((PARTS, 4, SOL + HALO), F32)]
    else:
        shapes = [jax.ShapeDtypeStruct((8, ATOMS), F32)] + [jax.ShapeDtypeStruct((4, HALO), F32)] * 2
    if gathers:
        scratch.append(pltpu.VMEM((3, NB, BLOCK), F32))
    if kicked:
        scratch.append(pltpu.VMEM((3, NB, BLOCK), F32))
    return pl.pallas_call(
        functools.partial(pair_kernel, step, kicked, gathers, last, halo[0] is halo[1]),
        out_shape=shapes,
        in_specs=specs,
        out_specs=[VMEM] * len(shapes),
        scratch_shapes=scratch,
        compiler_params=PARAMS,
        cost_estimate=pl.CostEstimate(flops=6_000_000_000, bytes_accessed=2_000_000, transcendentals=4_000_000),
        name="pair_step",
    )(*operands)


def double(cos, sin):
    twice = sin + sin
    return 1.0 - twice * sin, twice * cos


def product(a, b):
    return a[0] * b[0] - a[1] * b[1], a[1] * b[0] + a[0] * b[1]


def product_conj(a, b):
    return a[0] * b[0] + a[1] * b[1], a[1] * b[0] - a[0] * b[1]


def unit_powers(turns):
    y = (turns - jnp.round(turns)) * (0.5 * math.pi)
    z = y * y
    sin = ((-1.9515295891e-4 * z + 8.3321608736e-3) * z - 1.6666654611e-1) * (z * y) + y
    cos = ((2.443315711809948e-5 * z - 1.388731625493765e-3) * z + 4.166664568298827e-2) * (z * z) + (1.0 - 0.5 * z)
    one = double(*double(cos, sin))
    two = double(*one)
    three = product(two, one)
    five = product(three, two)
    seven = product(five, two)
    sixteen = double(*double(*double(*two)))
    return [one, three, five, seven], sixteen, product(double(*sixteen), seven)


def term_rows(powers):
    values = [p[0] for p in powers] + [p[1] for p in powers]
    parts = [halves(jnp.concatenate(values[i : i + 2], axis=0)) for i in range(0, 8, 2)]
    return [p[0] for p in parts], [p[1] for p in parts]


def group_directions(dir_ref, group):
    return [jnp.broadcast_to(dir_ref[0, 0, :, 16 * c + group : 16 * c + group + 1], (8, 128)) for c in range(3)]


def group_turns(u, point_ref, part, half):
    lanes = slice(half * 128, half * 128 + 128)

    def coordinate(c):
        return jnp.broadcast_to(point_ref[part, c : c + 1, lanes], (8, 128))

    return u[0] * coordinate(0) + u[1] * coordinate(1) + u[2] * coordinate(2), coordinate(3)


def shell_of(down, k, o):
    return 8 * k + 3 - o if down else 8 * k + 4 + o


def amplitude_kernel(position_ref, point_ref, dir_ref, amp_ref, inten_ref, total_ref):
    row = rows_of((8, 128))
    lane = lax.broadcasted_iota(jnp.int32, (8, 128), 1)

    turn = pl.program_id(0)
    for slot in range(SLOTS):
        u = group_directions(dir_ref, slot)
        total = None
        for at in chunks_of(slot):
            left = []
            right = []
            for n in range(CHUNK):
                turns, weight = group_turns(u, point_ref, part_of(turn, slot, at, n), n % 2)
                powers, step, start = unit_powers(turns)
                high, low = term_rows(powers)
                right.append(jnp.concatenate(high + low, axis=0))
                c, s = weight * start[0], weight * start[1]
                cb, sb = product_conj((c, s), step)
                twice = step[0] + step[0]
                tops = []
                bottoms = []
                for k in range(CENTERS):
                    top, bottom = halves(jnp.concatenate([c, s], axis=0))
                    tops.append(top)
                    bottoms.append(bottom)
                    if k + 1 < CENTERS:
                        c, s, cb, sb = twice * c - cb, twice * s - sb, c, s
                left.append(jnp.concatenate(tops + bottoms, axis=0))
            part = lax.dot_general(
                jnp.concatenate(left, axis=1),
                jnp.concatenate(right, axis=1),
                (((1,), (1,)), ((), ())),
                preferred_element_type=F32,
            )
            total = part if total is None else total + part
        total_ref[turn * SLOTS + slot] = total[0 : 16 * CENTERS] + total[16 * CENTERS :]

    @pl.when(turn == STEPS - 1)
    def _():
        own = (lane & 7) == row
        front = lane < 8 * SIDE
        squares = [jnp.zeros((8, 128), F32)] * 2
        for g in range(GROUPS):
            if g < GROUPS - 1:
                sums = total_ref[g // FULL * SLOTS + g % FULL]
            else:
                sums = total_ref[FULL] + total_ref[SLOTS + FULL]
            real = jnp.zeros((8, 128), F32)
            imag = real
            for k in range(CENTERS):
                c = jnp.sum(jnp.where(own, sums[16 * k : 16 * k + 8], 0.0), axis=0, keepdims=True)
                s = jnp.sum(jnp.where(own, sums[16 * k + 8 : 16 * k + 16], 0.0), axis=0, keepdims=True)
                real = jnp.where(row == k, c, real)
                imag = jnp.where(row == k, s, imag)
            real = (real + pltpu.roll(real, 64, axis=1)) * NORM
            imag = (imag + pltpu.roll(imag, 64, axis=1)) * NORM
            real_sin = pltpu.roll(real, 96, axis=1)
            imag_sin = pltpu.roll(imag, 96, axis=1)
            planes = [real - imag_sin, real + imag_sin, imag + real_sin, imag - real_sin]
            inside = front & ((lane & 7) + g * 8 < DIR_PART)
            planes = [jnp.where(inside, p, 0.0) for p in planes]
            for i in range(4):
                amp_ref[g, i] = planes[i]
            for i in range(2):
                squares[i] = squares[i] + planes[i] * planes[i] + planes[i + 2] * planes[i + 2]
        spread = jnp.zeros((1, 128), F32)
        for i in range(2):
            square = squares[i]
            for shift in (1, 2, 4):
                square = square + pltpu.roll(square, 128 - shift, axis=1)
            for k in range(CENTERS):
                for o in range(SIDE):
                    spread = jnp.where(lane[0:1] == shell_of(i, k, o), square[k : k + 1, 8 * o : 8 * o + 1], spread)
        inten_ref[...] = jnp.broadcast_to(spread, inten_ref.shape)


def chunks_of(slot):
    return range(LANE_GROUPS // CHUNK if slot < FULL else LANE_GROUPS // CHUNK // STEPS)


def part_of(turn, slot, at, n):
    part = (at * CHUNK + n) // 2
    return part if slot < FULL else turn * (PARTS // STEPS) + part


def point_spec():
    return pl.BlockSpec((PARTS, 4, SOL), lambda g, p: (0, 0, 0))


def direction_spec():
    return pl.BlockSpec((1, 1, 8, 128), lambda g, p: (p[0], g, 0, 0))


def amplitudes(position, points, directions):
    return pl.pallas_call(
        amplitude_kernel,
        grid_spec=pltpu.PrefetchScalarGridSpec(
            num_scalar_prefetch=1,
            grid=(STEPS,),
            in_specs=[point_spec(), direction_spec()],
            out_specs=[
                pl.BlockSpec((GROUPS, 4, 8, 128), lambda g, p: (0, 0, 0, 0)),
                pl.BlockSpec((PARTS * REPLICAS, 128), lambda g, p: (0, 0)),
            ],
            scratch_shapes=[pltpu.VMEM((STEPS * SLOTS, 16 * CENTERS, 128), F32)],
        ),
        out_shape=[
            jax.ShapeDtypeStruct((GROUPS, 4, 8, 128), F32),
            jax.ShapeDtypeStruct((PARTS * REPLICAS, 128), F32),
        ],
        compiler_params=PARAMS,
        cost_estimate=pl.CostEstimate(flops=10_000_000_000, bytes_accessed=1_000_000, transcendentals=0),
        name="amplitudes",
    )(position, points, directions)


def kick_kernel(position_ref, point_ref, dir_ref, amp_ref, inten_ref, precision_ref, target_ref, out_ref, coef_ref, acc_ref):
    row = rows_of((8, 128))
    lane = lax.broadcasted_iota(jnp.int32, (8, 128), 1)

    @pl.when(pl.program_id(0) == 0)
    def _():
        intensity = jnp.sum(inten_ref[...], axis=0, keepdims=True) * (1.0 / (M * REPLICAS))
        q = 1.0 + lax.broadcasted_iota(jnp.int32, (1, NQ), 1).astype(F32) * (3.0 / NQ)
        factor = precision_ref[...] * (intensity[:, 0:NQ] - target_ref[...]) * (2.0 / M) * q
        scales = []
        for i in range(2):
            scale = jnp.zeros((8, 128), F32)
            for k in range(CENTERS):
                for o in range(SIDE):
                    source = shell_of(i, k, o)
                    here = (row == k) & (lax.shift_right_logical(lane, 3) == o)
                    scale = jnp.where(here, jnp.broadcast_to(factor[:, source : source + 1], (8, 128)), scale)
            scales.append(scale)
        front = lane < 8 * SIDE
        own = (lane & 7) == row
        for g in range(GROUPS):
            b_up = amp_ref[g, 0] * scales[0]
            b_down = amp_ref[g, 1] * scales[1]
            a_up = amp_ref[g, 2] * scales[0]
            a_down = amp_ref[g, 3] * scales[1]
            real = jnp.where(front, a_up + a_down, pltpu.roll(b_down - b_up, 32, axis=1))
            imag = jnp.where(front, b_up + b_down, pltpu.roll(a_up - a_down, 32, axis=1))
            tops = []
            bottoms = []
            for v in (real, imag):
                high = v.astype(BF16).astype(F32)
                tops.append(high + pltpu.roll(high, 64, axis=1))
                bottoms.append(v - high)
            for k in range(CENTERS):
                at = slice(16 * k, 16 * k + 16)
                first = jnp.concatenate([jnp.where(own, v[k : k + 1], 0.0) for v in tops], axis=0).astype(BF16)
                last = jnp.concatenate([jnp.where(own, v[k : k + 1], 0.0) for v in bottoms], axis=0).astype(BF16)
                coef_ref[g, at, 0:128] = first
                coef_ref[g, at, 128:256] = last

    kicked = [[None] * 3 for _ in range(LANE_GROUPS)]
    halved = [[None] * 3 for _ in range(LANE_GROUPS // STEPS)]
    turn = pl.program_id(0)
    for slot in range(SLOTS):
        u = group_directions(dir_ref, slot)
        held = kicked if slot < FULL else halved
        group = turn * FULL + slot if slot < FULL else GROUPS - 1

        for at in chunks_of(slot):
            state = []
            columns = []
            for n in range(CHUNK):
                turns, _ = group_turns(u, point_ref, part_of(turn, slot, at, n), n % 2)
                powers, step, start = unit_powers(turns)
                high, low = term_rows(powers)
                columns.append(jnp.concatenate(high + low + high, axis=0))
                state.append([step, start, step[0] + step[0]])
            terms = jnp.dot(coef_ref[group, :, 0:192], jnp.concatenate(columns, axis=1), preferred_element_type=F32)
            for n in range(CHUNK):
                step, start, twice = state[n]
                lanes = slice(n * 128, n * 128 + 128)
                r1 = i1 = r2 = i2 = None
                for k in range(CENTERS - 1, -1, -1):
                    real = terms[16 * k : 16 * k + 8, lanes]
                    imag = terms[16 * k + 8 : 16 * k + 16, lanes]
                    if r1 is not None:
                        real = real + twice * r1
                        imag = imag + twice * i1
                    if r2 is not None:
                        real = real - r2
                        imag = imag - i2
                    r1, i1, r2, i2 = real, imag, r1, i1
                real = r1 - r2 * step[0] - i2 * step[1]
                imag = i1 - i2 * step[0] + r2 * step[1]
                slope = real * start[0] - imag * start[1]
                for c in range(3):
                    value = u[c] * slope
                    old = held[at * CHUNK + n][c]
                    held[at * CHUNK + n][c] = value if old is None else old + value

    @pl.when(turn == 0)
    def _():
        for j in range(LANE_GROUPS):
            for c in range(3):
                acc_ref[3 * j + c] = kicked[j][c]

    for j in range(LANE_GROUPS // STEPS):
        for c in range(3):
            acc_ref[3 * (turn * (LANE_GROUPS // STEPS) + j) + c] += halved[j][c]

    @pl.when(turn == STEPS - 1)
    def _():
        for j in range(LANE_GROUPS):
            lanes = slice(j % 2 * 128, j % 2 * 128 + 128)
            for c in range(3):
                total = acc_ref[3 * j + c] + kicked[j][c]
                out_ref[j // 2, c : c + 1, lanes] = jnp.sum(total, axis=0, keepdims=True) * (1.0 / TURN)


def kicks(position, points, directions, amplitude, intensity, shells):
    return pl.pallas_call(
        kick_kernel,
        grid_spec=pltpu.PrefetchScalarGridSpec(
            num_scalar_prefetch=1,
            grid=(STEPS,),
            in_specs=[
                point_spec(),
                direction_spec(),
                pl.BlockSpec((GROUPS, 4, 8, 128), lambda g, p: (0, 0, 0, 0)),
                pl.BlockSpec((PARTS * REPLICAS, 128), lambda g, p: (0, 0)),
                pl.BlockSpec((1, NQ), lambda g, p: (0, 0)),
                pl.BlockSpec((1, NQ), lambda g, p: (0, 0)),
            ],
            out_specs=pl.BlockSpec((PARTS, 3, SOL), lambda g, p: (0, 0, 0)),
            scratch_shapes=[
                pltpu.VMEM((GROUPS, 16 * CENTERS, 256), BF16),
                pltpu.VMEM((LANE_GROUPS * 3, 8, 128), F32),
            ],
        ),
        out_shape=jax.ShapeDtypeStruct((PARTS, 3, SOL), F32),
        compiler_params=PARAMS,
        cost_estimate=pl.CostEstimate(flops=10_000_000_000, bytes_accessed=1_000_000, transcendentals=0),
        name="kicks",
    )(position, points, directions, amplitude, intensity, *shells)


def exchange(head, tail):
    right = [(i, (i + 1) % PARTS) for i in range(PARTS)]
    left = [((i + 1) % PARTS, i) for i in range(PARTS)]
    return lax.ppermute(tail, "sp", right), lax.ppermute(head, "sp", left)


def to_all(value, axes):
    return lax.all_to_all(value, axes, 0, 0, tiled=True)


def shards(
    positions,
    velocities,
    strength,
    inv_mass,
    tile_lists,
    solute_index,
    scatter_weight,
    intensity_exp,
    precision,
):
    position = lax.axis_index("sp").astype(jnp.int32).reshape(1)
    directions = jnp.asarray(direction_table())
    usual = 3 * (jnp.arange(NB, dtype=jnp.int32) + HB)
    tiles = (jnp.sum(tile_lists[0], axis=-1) - usual).reshape(-1)
    shells = (precision.reshape(1, NQ), intensity_exp.reshape(1, NQ))
    state, head, tail, first = pack(
        positions[0], strength, velocities[0], inv_mass, solute_index, scatter_weight
    )
    halo = exchange(head, tail)
    first, halo = lax.optimization_barrier((first, halo))
    first = to_all(first, "sp")
    state, head, tail = pair_step(0, tiles, position, state, halo)
    halo = exchange(head, tail)
    amp, inten = amplitudes(position, first, directions)
    inten = to_all(inten, ("rep", "sp"))
    state, second = pair_step(
        1, tiles, position, state, halo, solute_index, scatter_weight, gathers=True
    )
    second = to_all(second, "sp")
    halo = (second, second)
    kick = to_all(kicks(position, first, directions, amp, inten, shells), "sp")
    amp, inten = amplitudes(position, second, directions)
    inten = to_all(inten, ("rep", "sp"))
    state, head, tail = pair_step(2, tiles, position, state, halo, solute_index, scatter_weight, kick)
    halo = exchange(head, tail)
    kick = to_all(kicks(position, second, directions, amp, inten, shells), "sp")
    place, speed = pair_step(3, tiles, position, state, halo, last=True)
    speed = finish(speed, inv_mass, solute_index, scatter_weight, kick)
    return (place[None], speed[None])


def solution(mesh):
    in_specs = (
        P("rep", None, "sp"),
        P("rep", None, "sp"),
        P("rep", "sp"),
        P("rep", "sp"),
        P("rep", None, "sp", None),
        P("rep", "sp"),
        P("rep", "sp"),
        P(),
        P(),
    )
    out_specs = (P("rep", None, "sp"), P("rep", None, "sp"))
    return jax.shard_map(shards, mesh=mesh, in_specs=in_specs, out_specs=out_specs, check_vma=False)
```
